32 devices in a mesh: dom: 8 (over y, x, core), tile: 4 (over z).
Axes of the slice: x: 2, y: 2, z: 4, core: 2. Of those that a mesh axis runs over, the one named last changes fastest.
Arguments:
- vorticity: float32 [32, 2, 64, 2048], P('dom', None, 'tile'), may hold values from -6 to 6
- streamfunction: float32 [32, 2, 64, 2048], P('dom', None, 'tile'), may hold values from -6 to 6
- model_noise: float32 [2, 32, 2, 64, 2048], P(None, 'dom', None, 'tile'), may hold values from -3 to 3
- offspring: int32 [2, 32], replicated, may hold values from 0 to 8, as said below
- footprint: float32 [8, 16, 1024, 1024], P('tile', 'dom'), may hold values from -0.1875 to 0.1875
- observed: float32 [8, 16, 1024], P('tile', 'dom'), may hold values from -6 to 6
- precision: float32 [8, 16, 1024], P('tile', 'dom'), may hold values from 0.002 to 0.02
- block_rows: int32 [8, 16], P('tile', 'dom'), may hold values from 0 to 8
Outputs:
- vorticity_out: float32 [32, 2, 64, 2048], P('dom', None, 'tile')
- streamfunction_out: float32 [32, 2, 64, 2048], P('dom', None, 'tile')
- mean_loglik: float32 [2, 32], replicated
- weights: float32 [2, 32], replicated
The draws below stay inside these ranges and needn't reach their ends.
Inputs may be any that keep to these rules, and one draw needn't show every extreme that they name: Each row sums to 32; in each row exactly one member has 8 offspring.
All inputs are finite; a program needn't handle non-finite values.
Results may differ from the reference program's by a relative error of at most 0.00055.
Values sent between devices are 32-bit elements; how exact they have to be, the bound alone decides.
No kernel may reach another device: no remote copies, remote signals or barrier semaphores. Data moves between devices by JAX's collectives and lax.ppermute only.
A program may use at most 192 MiB of HBM per device.

```python
import math
import jax
import jax.numpy as jnp
from jax import lax

P_SIZE = 32
NX = 2048
TROWS = 16
NY = 64
STEPS = 6
CYCLES = 2
BW = 128
BR = 8
OPB = 1024
BT = 2
NBR = 8
NBC = 16
K = 1024
NOBS = 131072


def child_particle_row(key):
    most = P_SIZE // 4
    keys = jax.random.split(key, 2)
    favored = jax.random.randint(keys[0], (), 0, P_SIZE)
    order = jax.random.permutation(keys[1], P_SIZE * most)
    owner = (order // most).astype(jnp.int32)
    usable = (owner != favored).astype(jnp.int32)
    ranked = jnp.cumsum(usable)
    taken = usable * (ranked <= P_SIZE - most).astype(jnp.int32)
    ensemble_size = jnp.arange(P_SIZE, dtype=jnp.int32)
    counts = jnp.sum(taken[None, :] * (owner[None, :] == ensemble_size[:, None]).astype(jnp.int32), axis=1)
    return (counts + most * (ensemble_size == favored).astype(jnp.int32)).astype(jnp.int32)


def draw_offspring(key, part):
    keys = jax.random.split(key, CYCLES)
    return jax.vmap(child_particle_row)(keys).astype(jnp.int32)


def set_ends(drawn, stream_key, smallest, largest):
    extent = drawn.shape
    spot = [jax.random.randint(jax.random.fold_in(stream_key, axis), (), 0, extent[axis]) for axis in range(len(extent))]
    drawn = drawn.at[tuple(spot)].set(smallest)
    longest = extent.index(max(extent))
    spot[longest] = (spot[longest] + 1) % extent[longest]
    return drawn.at[tuple(spot)].set(largest)


def block_levels(rng, dims, cuts, least, top_value):
    level = 1.0
    for axis_at, blocks in cuts:
        steps = jax.random.uniform(jax.random.fold_in(jax.random.fold_in(rng, 6), axis_at), (blocks,), jnp.float32, least / len(cuts), top_value / len(cuts))
        level = level * jnp.repeat(jnp.exp(steps), dims[axis_at] // blocks).reshape((-1,) + (1,) * (len(dims) - 1 - axis_at))
    return level


def scatter_about(stream_key, dims, spread, bound, cuts=(), kind=jnp.bfloat16):
    values = spread * jax.random.normal(stream_key, dims, jnp.float32)
    if cuts:
        values = values * block_levels(stream_key, dims, cuts, -0.22, 0.18)
    return jnp.clip(values, -bound, bound).astype(kind)


def setup_inputs(seed: int = 0) -> dict:
    streams_of = jax.random.split(jax.random.key(seed), 9)
    vorticity = scatter_about(streams_of[0], (P_SIZE, 2, NY, NX), 1.0, 6.0, ((0, 8), (2, 4)), jnp.float32)
    streamfunction = scatter_about(streams_of[1], (P_SIZE, 2, NY, NX), 1.0, 6.0, ((0, 8), (2, 4)), jnp.float32)
    model_noise = scatter_about(streams_of[2], (CYCLES, P_SIZE, 2, NY, NX), 0.5, 3.0, ((1, 8), (3, 4)), jnp.float32)
    offspring = draw_offspring(jax.random.fold_in(streams_of[8], 71), 0)
    footprint = scatter_about(streams_of[4], (NBR, NBC, OPB, K), K ** -0.5, 0.1875, ((0, 4), (1, 8)), jnp.float32)
    observed = scatter_about(streams_of[5], (NBR, NBC, OPB), 1.0, 6.0, ((0, 4), (1, 8)), jnp.float32)
    precision = jnp.clip(jnp.exp(math.log(0.02) - 2.30258502 * jax.random.uniform(streams_of[6], (NBR, NBC, OPB), jnp.float32) ** block_levels(streams_of[6], (NBR, NBC, OPB), ((0, 4), (1, 8)), -0.2, 0.2)), 0.002, 0.02)
    block_rows = set_ends(jax.random.randint(streams_of[7], (NBR, NBC), 0, TROWS - BR + 1), jax.random.fold_in(streams_of[7], 1), 0, TROWS - BR).astype(jnp.int32)
    return dict(vorticity=vorticity, streamfunction=streamfunction, model_noise=model_noise, offspring=offspring, footprint=footprint, observed=observed, precision=precision, block_rows=block_rows)


INTERFACE_LINK = 1.0
BETA = 0.5
DRAG = 0.2
TIME_STEP = 0.1


def advance(padded, column_pad):
    vortex = padded[..., 0, :, :, :]
    stream = padded[..., 1, :, :, :]

    def neighbours(field):
        if column_pad:
            middle = field[..., 1:-1, 1:-1]
            north = field[..., 2:, 1:-1]
            south = field[..., :-2, 1:-1]
            east = field[..., 1:-1, 2:]
            west = field[..., 1:-1, :-2]
        else:
            middle = field[..., 1:-1, :]
            north = field[..., 2:, :]
            south = field[..., :-2, :]
            east = jnp.roll(middle, -1, -1)
            west = jnp.roll(middle, 1, -1)
        return middle, north, south, east, west

    vortex_mid, vortex_north, vortex_south, vortex_east, vortex_west = neighbours(vortex)
    stream_mid, stream_north, stream_south, stream_east, stream_west = neighbours(stream)
    other = stream_mid[..., ::-1, :, :]
    beside_all = stream_north + stream_south + stream_east + stream_west
    stream_new = (beside_all + INTERFACE_LINK * other - vortex_mid) / (4.0 + INTERFACE_LINK)
    jacobian = ((stream_east - stream_west) * (vortex_north - vortex_south)
                - (stream_north - stream_south) * (vortex_east - vortex_west)) * 0.25
    layer_mask = jnp.array([0.0, 1.0], jnp.float32)[:, None, None]
    friction = DRAG * layer_mask * (beside_all - 4.0 * stream_mid)
    updated_vorticity = vortex_mid - TIME_STEP * (jacobian + BETA * 0.5 * (stream_east - stream_west) + friction)
    return jnp.stack((updated_vorticity, stream_new), axis=-4)


def ancestry(counts):
    running = jnp.cumsum(counts)
    slots = jnp.arange(counts.shape[0], dtype=jnp.int32)
    return jnp.sum((running[None, :] <= slots[:, None]).astype(jnp.int32), axis=1).astype(jnp.int32)


def run_member(member):
    for step in range(STEPS):
        padded = jnp.pad(member, ((0, 0), (0, 0), (1, 1), (0, 0)))
        member = advance(padded, False)
    return member


def likelihood(surface, footprint, observed, precision, block_rows):
    def block_term(total, index):
        row_block = index // NBC
        col_block = index % NBC
        leading_line_index = ((row_block // BT) * TROWS + block_rows[row_block, col_block]).astype(jnp.int32)
        first_col = (col_block * BW).astype(jnp.int32)
        patch = lax.dynamic_slice(surface, (jnp.int32(0), leading_line_index, first_col), (P_SIZE, BR, BW))
        flat = patch.reshape(P_SIZE, K)
        predicted = lax.dot_general(flat, footprint[row_block, col_block], (((1,), (1,)), ((), ())),
                                    precision=lax.Precision.HIGHEST, preferred_element_type=jnp.float32)
        miss = observed[row_block, col_block][None, :] - predicted
        total = total + jnp.sum(precision[row_block, col_block][None, :] * miss * miss, axis=1)
        return total, None

    total, unused = lax.scan(block_term, jnp.zeros((P_SIZE,), jnp.float32), jnp.arange(NBR * NBC, dtype=jnp.int32))
    return -0.5 * total


def reference(vorticity, streamfunction, model_noise, offspring, footprint, observed, precision, block_rows):
    sample_vector = jnp.stack((vorticity, streamfunction), axis=1)
    logs = []
    for cycle in range(CYCLES):
        sample_vector = sample_vector.at[:, 0].add(model_noise[cycle])
        sample_vector = lax.map(run_member, sample_vector)
        logs.append(likelihood(sample_vector[:, 1, 0], footprint, observed, precision, block_rows))
        sample_vector = jnp.take(sample_vector, ancestry(offspring[cycle]), axis=0)
    loglik = jnp.stack(logs)
    mean_loglik = loglik / NOBS
    highest = jnp.max(loglik, axis=1, keepdims=True)
    scaled = jnp.exp(loglik - highest)
    weights = scaled / jnp.sum(scaled, axis=1, keepdims=True)
    return sample_vector[:, 0], sample_vector[:, 1], mean_loglik, weights
```

```python
import functools

import jax
import jax.numpy as jnp
from jax import lax
from jax.experimental import pallas as pl
from jax.experimental.pallas import tpu as pltpu
from jax.sharding import PartitionSpec as P

STEPS = 6
CYCLES = 2
BW = 128
BR = 8
ROWS = 16
MEM = 4
LAYERS = 2
SUB = 8
SEG = 16
F32 = jnp.float32
VMEM_LIMIT = 56 * 1024 * 1024
DRAG_STEP = 0.1 * 0.2


def lanes():
    return lax.broadcasted_iota(jnp.int32, (SUB, BW), 1)


def lane_roll(x, shift):
    return pltpu.roll(x, shift % BW, axis=1)


def ring_row(blocks, load, other, emit, drag):
    lane = lanes()
    at_last, at_first = lane == BW - 1, lane == 0
    cur = (load(1, 0, 0), load(0, 0, 0))
    left = tuple(lane_roll(v, -1) for v in cur)
    right = tuple(lane_roll(v, 1) for v in cur)
    first_left = left
    before = tuple(lane_roll(load(f, blocks - 1, 0), 1) for f in (1, 0))
    for b in range(blocks):
        if b + 1 < blocks:
            nxt = (load(1, b + 1, 0), load(0, b + 1, 0))
            nxt_left = tuple(lane_roll(v, -1) for v in nxt)
            nxt_right = tuple(lane_roll(v, 1) for v in nxt)
        else:
            nxt, nxt_left, nxt_right = None, first_left, None
        psi, q = cur
        psi_e, q_e = (jnp.where(at_last, n, c) for n, c in zip(nxt_left, left))
        psi_w, q_w = (jnp.where(at_first, p, c) for p, c in zip(before, right))
        psi_n, psi_s = load(1, b, 1), load(1, b, -1)
        q_n, q_s = load(0, b, 1), load(0, b, -1)
        around = (psi_n + psi_s) + (psi_e + psi_w)
        along = psi_e - psi_w
        psi_new = (around + other(b, psi) - q) * 0.2
        change = along * ((q_n - q_s) + 1.0) - (psi_n - psi_s) * (q_e - q_w)
        q_new = q - 0.025 * change
        if drag is not None:
            q_new = q_new - drag * (around - 4.0 * psi)
        emit(b, q_new, psi_new)
        before = right
        cur, left, right = nxt, nxt_left, nxt_right


def halo_pack(take, rows):
    segment = ((lanes() + SEG // 2) // SEG) % SUB
    lower = lanes() < BW // 2
    packed = None
    for j in range(rows):
        before, after = take(j)
        edge = lane_roll(jnp.where(lower, after, before), SEG * j)
        packed = edge if packed is None else jnp.where(segment == j, edge, packed)
    return packed


def pack_state(q_ref, p_ref, n_ref, main_ref, up_ref, down_ref, *, blocks):
    for b in range(blocks):
        cols = slice(b * BW, (b + 1) * BW)
        for m in range(MEM):
            for l in range(LAYERS):
                for g in range(ROWS // SUB):
                    rows = slice(g * SUB, (g + 1) * SUB)
                    start = g * SUB * 16 + l * MEM + m
                    main_ref[b, pl.ds(start, SUB, stride=16), :] = (
                        q_ref[m, l, rows, cols] + n_ref[0, m, l, rows, cols]
                    )
                    main_ref[b, pl.ds(start + SUB, SUB, stride=16), :] = p_ref[m, l, rows, cols]
        up_ref[b] = main_ref[b, (ROWS - STEPS) * 16 :, :]
        down_ref[b] = main_ref[b, : STEPS * 16, :]


def pack_noise(n_ref, out_ref, work, edges, *, groups, per):
    blocks = groups * per
    for b in range(blocks):
        for m in range(MEM):
            for l in range(LAYERS):
                for g in range(ROWS // SUB):
                    work[b, pl.ds(g * SUB * SUB + l * MEM + m, SUB, stride=SUB), :] = n_ref[
                        0, m, l, g * SUB : (g + 1) * SUB, b * BW : (b + 1) * BW
                    ]
    for d in range(groups):
        for h in range(2):
            def take(j):
                row = slice((h * SUB + j) * SUB, (h * SUB + j + 1) * SUB)
                return work[(d * per - 1) % blocks, row, :], work[(d * per + per) % blocks, row, :]

            edges[d, h * 16 : h * 16 + SUB, :] = halo_pack(take, SUB)
            edges[d, h * 16 + SUB : (h + 1) * 16, :] = jnp.zeros((SUB, BW), F32)
        for m in range(MEM):
            for c in range(per):
                for v in range(4):
                    out_ref[d, m, c * 4 + v] = work[d * per + c, pl.ds(v * 32 + m, SUB, stride=MEM), :]
            out_ref[d, m, per * 4] = edges[d, pl.ds(m, SUB, stride=MEM), :]


def clear_wall(buf, row, planes, edge):
    zero = jnp.zeros((STEPS * row, BW), F32)

    @pl.when(edge[0] == 0)
    def _():
        for b in range(planes):
            buf[b, : STEPS * row, :] = zero

    @pl.when(edge[0] == edge[1] - 1)
    def _():
        for b in range(planes):
            buf[b, (STEPS + ROWS) * row :, :] = zero


def row_range(edge, step):
    low = jnp.where(edge[0] == 0, STEPS, step + 1)
    high = jnp.where(edge[0] == edge[1] - 1, STEPS + ROWS, 2 * STEPS + ROWS - 1 - step)
    return low, high


def advance_members(edge, main_ref, up_ref, down_ref, out_ref, first, second, edges, *, groups, per):
    blocks = groups * per
    row = 2 * SUB
    for b in range(blocks):
        first[b, : STEPS * row, :] = up_ref[b]
        first[b, STEPS * row : (STEPS + ROWS) * row, :] = main_ref[b]
        first[b, (STEPS + ROWS) * row :, :] = down_ref[b]
    clear_wall(second, row, blocks, edge)
    drag = jnp.where(lax.broadcasted_iota(jnp.int32, (SUB, BW), 0) >= MEM, DRAG_STEP, 0.0).astype(F32)
    src, dst = first, second
    for step in range(STEPS):
        def body(i, _, src=src, dst=dst):
            def at(f, di):
                return pl.ds(pl.multiple_of((i + di) * row + f * SUB, SUB), SUB)

            def emit(b, q_new, psi_new):
                dst[b, at(0, 0), :] = q_new
                dst[b, at(1, 0), :] = psi_new

            ring_row(
                blocks,
                lambda f, b, di: src[b, at(f, di), :],
                lambda b, psi: pltpu.roll(psi, MEM, axis=0),
                emit,
                drag,
            )
            return 0

        low, high = row_range(edge, step)
        lax.fori_loop(low, high, body, 0)
        src, dst = dst, src
    base = STEPS * row
    for d in range(groups):
        for h in range(2):
            for f in range(2):
                def take(j):
                    s = base + (h * SUB + j) * row + f * SUB
                    rows = slice(s, s + SUB)
                    return src[(d * per - 1) % blocks, rows, :], src[(d * per + per) % blocks, rows, :]

                edges[d, (h * 2 + f) * SUB : (h * 2 + f + 1) * SUB, :] = halo_pack(take, SUB)
        for m in range(MEM):
            for c in range(per):
                for v in range(8):
                    out_ref[d, m, c * 8 + v] = src[
                        d * per + c, pl.ds(base + v * 32 + m, SUB, stride=MEM), :
                    ]
            out_ref[d, m, per * 8] = edges[d, pl.ds(m, SUB, stride=MEM), :]


def resample(
    parent, x_ref, n_ref, main_ref, edge_ref, up_ref, down_ref, z_ref, noise, *, members, per
):
    size = per * 8 + 1
    row = 4 * members

    def one(k, _):
        p = parent[k]
        for c in range(per):
            for v in range(8):
                main_ref[c, pl.ds(v * 8 * members + k, SUB, stride=members), :] = x_ref[p, c * 8 + v]
            for v in range(4):
                noise[c, pl.ds(v * 8 * members + k, SUB, stride=members), :] = n_ref[k, c * 4 + v]
            for g in range(2):
                for r in range(SUB):
                    j = g * SUB + r
                    z_ref[c, pl.ds(j * members + k, 1), :] = x_ref[
                        k, c * 8 + j // 2, (j % 2) * 4 + 2 : (j % 2) * 4 + 3, :
                    ]
        edge_ref[pl.ds(k, SUB, stride=members), :] = x_ref[p, size - 1] + n_ref[k, per * 4]
        return 0

    lax.fori_loop(0, members, one, 0)
    for c in range(per):
        for r in range(ROWS):
            s = slice(r * row, r * row + 2 * members)
            main_ref[c, s, :] = main_ref[c, s, :] + noise[c, r * 2 * members : (r + 1) * 2 * members, :]
        for r in range(STEPS):
            up_ref[c * STEPS + r] = main_ref[c, (ROWS - STEPS + r) * row : (ROWS - STEPS + r + 1) * row, :]
            down_ref[c * STEPS + r] = main_ref[c, r * row : (r + 1) * row, :]
    up_ref[per * STEPS] = edge_ref[row:, :]
    down_ref[per * STEPS] = edge_ref[:row, :]


def advance_columns(
    edge, parent, main_ref, edge_ref, up_ref, down_ref, out_ref, z_ref, first, second, *, members, per
):
    row = 4 * members
    top = (STEPS + ROWS) * row
    for c in range(per):
        for r in range(STEPS):
            first[c, r * row : (r + 1) * row, :] = up_ref[c * STEPS + r]
            first[c, top + r * row : top + (r + 1) * row, :] = down_ref[c * STEPS + r]
        first[c, STEPS * row : top, :] = main_ref[c]
    for j in range(SUB):
        for h in range(2):
            s = (STEPS + h * SUB + j) * row
            first[per, s : s + row, :] = lane_roll(edge_ref[h * row : (h + 1) * row, :], -SEG * j)
        if j >= SUB - STEPS:
            s = (j - (SUB - STEPS)) * row
            first[per, s : s + row, :] = lane_roll(up_ref[per * STEPS], -SEG * j)
        if j < STEPS:
            s = top + j * row
            first[per, s : s + row, :] = lane_roll(down_ref[per * STEPS], -SEG * j)
    clear_wall(second, row, per + 1, edge)
    src, dst = first, second
    for step in range(STEPS):
        def body(i, _, src=src, dst=dst):
            for g in range(members // SUB):
                for l in range(LAYERS):
                    def at(f, layer, di):
                        s = (i + di) * row + (f * 2 + layer) * members + g * SUB
                        return pl.ds(pl.multiple_of(s, SUB), SUB)

                    def emit(b, q_new, psi_new):
                        dst[b, at(0, l, 0), :] = q_new
                        dst[b, at(1, l, 0), :] = psi_new

                    ring_row(
                        per + 1,
                        lambda f, b, di: src[b, at(f, l, di), :],
                        lambda b, psi: src[b, at(1, 1 - l, 0), :],
                        emit,
                        DRAG_STEP if l == 1 else None,
                    )
            return 0

        low, high = row_range(edge, step)
        lax.fori_loop(low, high, body, 0)
        src, dst = dst, src

    def one(k, _):
        p = parent[k]
        for c in range(per):
            for v in range(8):
                out_ref[k, c * 8 + v] = src[
                    c, pl.ds(STEPS * row + v * 8 * members + p, SUB, stride=members), :
                ]
        return 0

    lax.fori_loop(0, members, one, 0)
    for c in range(per):
        for r in range(ROWS):
            s = (STEPS + r) * row + 2 * members
            z_ref[c, r * members : (r + 1) * members, :] = src[c, s : s + members, :]


def unpack_state(y_ref, q_ref, p_ref, *, per):
    for c in range(per):
        for m in range(MEM):
            for l in range(LAYERS):
                for g in range(ROWS // SUB):
                    rows, cols = slice(g * SUB, (g + 1) * SUB), slice(c * BW, (c + 1) * BW)
                    s = c * 64 + g * 32 + l
                    q_ref[m, l, rows, cols] = y_ref[0, m, pl.ds(s, SUB, stride=4), :]
                    p_ref[m, l, rows, cols] = y_ref[0, m, pl.ds(s + 2, SUB, stride=4), :]


def score(rows_ref, z_ref, f_ref, o_ref, w_ref, out_ref, patch, total, *, members, per, chunk):
    a, c, j = pl.program_id(0), pl.program_id(1), pl.program_id(2)

    @pl.when((a == 0) & (c == 0) & (j == 0))
    def _():
        total[...] = jnp.zeros_like(total)

    @pl.when(j == 0)
    def _():
        start = rows_ref[a, c]
        for r in range(BR):
            s = pl.multiple_of((start + r) * members, SUB)
            part = z_ref[c, pl.ds(s, members), :]
            high = part.astype(jnp.bfloat16)
            patch[:members, r * BW : (r + 1) * BW] = high
            patch[members:, r * BW : (r + 1) * BW] = (part - high.astype(F32)).astype(jnp.bfloat16)

    weights = f_ref[0, 0]
    high = weights.astype(jnp.bfloat16)
    low = (weights - high.astype(F32)).astype(jnp.bfloat16)
    dims = (((1,), (1,)), ((), ()))
    main = lax.dot_general(patch[...], high, dims, preferred_element_type=F32)
    rest = lax.dot_general(patch[:members, :], low, dims, preferred_element_type=F32)
    predicted = main[:members] + (main[members:] + rest)
    miss = o_ref[0, 0] - predicted
    total[...] += w_ref[0, 0] * miss * miss

    @pl.when((a == pl.num_programs(0) - 1) & (c == pl.num_programs(1) - 1) & (j == pl.num_programs(2) - 1))
    def _():
        out_ref[...] = jnp.broadcast_to(jnp.sum(total[...], axis=1, keepdims=True) * -0.5, (members, BW))


def shape(*dims):
    return jax.ShapeDtypeStruct(dims, F32)


def call(kernel, outs, scratch=(), scalars=0, name=None):
    def run(*args):
        specs = [pl.BlockSpec(memory_space=pltpu.SMEM)] * scalars
        specs += [pl.BlockSpec(memory_space=pltpu.VMEM)] * (len(args) - scalars)
        return pl.pallas_call(
            kernel,
            out_shape=outs,
            in_specs=specs,
            out_specs=[pl.BlockSpec(memory_space=pltpu.VMEM)] * len(outs),
            scratch_shapes=list(scratch),
            compiler_params=pltpu.CompilerParams(vmem_limit_bytes=VMEM_LIMIT),
            name=name,
        )(*args)

    return run


def shards(
    vorticity, streamfunction, model_noise, offspring, footprint, observed, precision, block_rows
):
    groups, tiles = lax.axis_size("dom"), lax.axis_size("tile")
    members = offspring.shape[1]
    width = vorticity.shape[3]
    blocks = width // BW
    per = blocks // groups
    bands, observations, cells = footprint.shape[0], footprint.shape[2], footprint.shape[3]

    running = jnp.cumsum(offspring, axis=1)
    slots = jnp.arange(members, dtype=jnp.int32)
    parent = jnp.sum((running[:, None, :] <= slots[None, :, None]).astype(jnp.int32), axis=2)
    parent = jnp.minimum(parent, members - 1)
    edge = jnp.stack([lax.axis_index("tile"), jnp.int32(tiles)]).astype(jnp.int32)

    up = [(i, i + 1) for i in range(tiles - 1)]
    down = [(i + 1, i) for i in range(tiles - 1)]

    fields = (MEM, LAYERS, ROWS)
    step_blocks = blocks // 4
    main, to_up, to_down = pl.pallas_call(
        functools.partial(pack_state, blocks=step_blocks),
        grid=(4,),
        in_specs=[
            pl.BlockSpec(fields + (step_blocks * BW,), lambda i: (0, 0, 0, i)),
            pl.BlockSpec(fields + (step_blocks * BW,), lambda i: (0, 0, 0, i)),
            pl.BlockSpec((1,) + fields + (step_blocks * BW,), lambda i: (0, 0, 0, 0, i)),
        ],
        out_specs=[
            pl.BlockSpec((step_blocks, ROWS * 16, BW), lambda i: (i, 0, 0)),
            pl.BlockSpec((step_blocks, STEPS * 16, BW), lambda i: (i, 0, 0)),
            pl.BlockSpec((step_blocks, STEPS * 16, BW), lambda i: (i, 0, 0)),
        ],
        out_shape=[
            shape(blocks, ROWS * 16, BW),
            shape(blocks, STEPS * 16, BW),
            shape(blocks, STEPS * 16, BW),
        ],
        name="pack_state",
    )(vorticity, streamfunction, model_noise)
    from_below = lax.ppermute(to_up, "tile", up)
    from_above = lax.ppermute(to_down, "tile", down)

    noise = pl.pallas_call(
        functools.partial(pack_noise, groups=groups, per=per),
        grid=(1,),
        in_specs=[pl.BlockSpec((1,) + fields + (width,), lambda i: (1, 0, 0, 0, 0))],
        out_specs=pl.BlockSpec((groups, MEM, per * 4 + 1, SUB, BW), lambda i: (0, 0, 0, 0, 0)),
        out_shape=shape(groups, MEM, per * 4 + 1, SUB, BW),
        scratch_shapes=[pltpu.VMEM((blocks, ROWS * SUB, BW), F32), pltpu.VMEM((groups, 32, BW), F32)],
        name="pack_noise",
    )(model_noise)
    noise = lax.all_to_all(noise, "dom", split_axis=0, concat_axis=0, tiled=True)
    noise = noise.reshape(members, per * 4 + 1, SUB, BW)

    work = (blocks, (ROWS + 2 * STEPS) * 16, BW)
    (sent,) = call(
        functools.partial(advance_members, groups=groups, per=per),
        [shape(groups, MEM, per * 8 + 1, SUB, BW)],
        [pltpu.VMEM(work, F32), pltpu.VMEM(work, F32), pltpu.VMEM((groups, 32, BW), F32)],
        scalars=1,
        name="advance_members",
    )(edge, main, from_below, from_above)
    owned = lax.all_to_all(sent, "dom", split_axis=0, concat_axis=0, tiled=True)
    owned = owned.reshape(members, per * 8 + 1, SUB, BW)

    row = 4 * members
    main, sides, to_up, to_down, surface = call(
        functools.partial(resample, members=members, per=per),
        [
            shape(per, ROWS * row, BW),
            shape(2 * row, BW),
            shape(per * STEPS + 1, row, BW),
            shape(per * STEPS + 1, row, BW),
            shape(per, ROWS * members, BW),
        ],
        [pltpu.VMEM((per, ROWS * 2 * members, BW), F32)],
        scalars=1,
        name="resample",
    )(parent[0], owned, noise)
    from_below = lax.ppermute(to_up, "tile", up)
    from_above = lax.ppermute(to_down, "tile", down)

    def likelihood(surface):
        chunk = 512
        obs = (bands, per, 1, observations)
        out = pl.pallas_call(
            functools.partial(score, members=members, per=per, chunk=chunk),
            grid=(bands, per, observations // chunk),
            in_specs=[
                pl.BlockSpec(memory_space=pltpu.SMEM),
                pl.BlockSpec((per, ROWS * members, BW), lambda a, c, j: (0, 0, 0)),
                pl.BlockSpec((1, 1, chunk, cells), lambda a, c, j: (a, c, j, 0)),
                pl.BlockSpec((1, 1, 1, chunk), lambda a, c, j: (a, c, 0, j)),
                pl.BlockSpec((1, 1, 1, chunk), lambda a, c, j: (a, c, 0, j)),
            ],
            out_specs=pl.BlockSpec((members, BW), lambda a, c, j: (0, 0)),
            out_shape=shape(members, BW),
            scratch_shapes=[
                pltpu.VMEM((2 * members, cells), jnp.bfloat16),
                pltpu.VMEM((members, chunk), F32),
            ],
            compiler_params=pltpu.CompilerParams(vmem_limit_bytes=VMEM_LIMIT),
            name="score",
        )(block_rows, surface, footprint, observed.reshape(obs), precision.reshape(obs))
        return lax.psum(out[:, 0], ("dom", "tile"))

    logs = [likelihood(surface)]

    work = (per + 1, (ROWS + 2 * STEPS) * row, BW)
    back, surface = call(
        functools.partial(advance_columns, members=members, per=per),
        [shape(members, per * 8, SUB, BW), shape(per, ROWS * members, BW)],
        [pltpu.VMEM(work, F32), pltpu.VMEM(work, F32)],
        scalars=2,
        name="advance_columns",
    )(edge, parent[1], main, sides, from_below, from_above)
    back = back.reshape(groups, MEM, per * 64, BW)
    mine = lax.all_to_all(back, "dom", split_axis=0, concat_axis=0, tiled=True)
    logs.append(likelihood(surface))

    q_out, psi_out = pl.pallas_call(
        functools.partial(unpack_state, per=per),
        grid=(groups,),
        in_specs=[pl.BlockSpec((1, MEM, per * 64, BW), lambda i: (i, 0, 0, 0))],
        out_specs=[pl.BlockSpec(fields + (per * BW,), lambda i: (0, 0, 0, i))] * 2,
        out_shape=[shape(*fields, width)] * 2,
        name="unpack_state",
    )(mine)

    loglik = jnp.stack(logs)
    total_obs = observed.size * groups * tiles
    mean_loglik = loglik / total_obs
    highest = jnp.max(loglik, axis=1, keepdims=True)
    scaled = jnp.exp(loglik - highest)
    weights = scaled / jnp.sum(scaled, axis=1, keepdims=True)
    return (q_out, psi_out, mean_loglik, weights)


def solution(mesh):
    return jax.shard_map(
        shards,
        mesh=mesh,
        in_specs=(
            P("dom", None, "tile", None),
            P("dom", None, "tile", None),
            P(None, "dom", None, "tile", None),
            P(),
            P("tile", "dom", None, None),
            P("tile", "dom", None),
            P("tile", "dom", None),
            P("tile", "dom"),
        ),
        out_specs=(P("dom", None, "tile", None), P("dom", None, "tile", None), P(), P()),
        check_vma=False,
    )
```

```python
import functools

import jax
import jax.numpy as jnp
from jax import lax
from jax.experimental import pallas as pl
from jax.experimental.pallas import tpu as pltpu
from jax.sharding import PartitionSpec as P

STEPS = 6
CYCLES = 2
BW = 128
BR = 8
ROWS = 16
MEM = 4
LAYERS = 2
SUB = 8
SEG = 16
F32 = jnp.float32
VMEM_LIMIT = 56 * 1024 * 1024
DRAG_STEP = 0.1 * 0.2


def lanes():
    return lax.broadcasted_iota(jnp.int32, (SUB, BW), 1)


def lane_roll(x, shift):
    return pltpu.roll(x, shift % BW, axis=1)


def ring_row(blocks, load, other, emit, drag):
    lane = lanes()
    at_last, at_first = lane == BW - 1, lane == 0
    cur = (load(1, 0, 0), load(0, 0, 0))
    left = tuple(lane_roll(v, -1) for v in cur)
    right = tuple(lane_roll(v, 1) for v in cur)
    first_left = left
    before = tuple(lane_roll(load(f, blocks - 1, 0), 1) for f in (1, 0))
    for b in range(blocks):
        if b + 1 < blocks:
            nxt = (load(1, b + 1, 0), load(0, b + 1, 0))
            nxt_left = tuple(lane_roll(v, -1) for v in nxt)
            nxt_right = tuple(lane_roll(v, 1) for v in nxt)
        else:
            nxt, nxt_left, nxt_right = None, first_left, None
        psi, q = cur
        psi_e, q_e = (jnp.where(at_last, n, c) for n, c in zip(nxt_left, left))
        psi_w, q_w = (jnp.where(at_first, p, c) for p, c in zip(before, right))
        psi_n, psi_s = load(1, b, 1), load(1, b, -1)
        q_n, q_s = load(0, b, 1), load(0, b, -1)
        around = (psi_n + psi_s) + (psi_e + psi_w)
        along = psi_e - psi_w
        psi_new = (around + other(b, psi) - q) * 0.2
        change = along * ((q_n - q_s) + 1.0) - (psi_n - psi_s) * (q_e - q_w)
        q_new = q - 0.025 * change
        if drag is not None:
            q_new = q_new - drag * (around - 4.0 * psi)
        emit(b, q_new, psi_new)
        before = right
        cur, left, right = nxt, nxt_left, nxt_right


def halo_pack(take, rows):
    segment = ((lanes() + SEG // 2) // SEG) % SUB
    lower = lanes() < BW // 2
    packed = None
    for j in range(rows):
        before, after = take(j)
        edge = lane_roll(jnp.where(lower, after, before), SEG * j)
        packed = edge if packed is None else jnp.where(segment == j, edge, packed)
    return packed


def pack_state(q_ref, p_ref, n_ref, main_ref, up_ref, down_ref, *, blocks):
    for b in range(blocks):
        cols = slice(b * BW, (b + 1) * BW)
        for m in range(MEM):
            for l in range(LAYERS):
                for g in range(ROWS // SUB):
                    rows = slice(g * SUB, (g + 1) * SUB)
                    start = g * SUB * 16 + l * MEM + m
                    main_ref[b, pl.ds(start, SUB, stride=16), :] = (
                        q_ref[m, l, rows, cols] + n_ref[0, m, l, rows, cols]
                    )
                    main_ref[b, pl.ds(start + SUB, SUB, stride=16), :] = p_ref[m, l, rows, cols]
        up_ref[b] = main_ref[b, (ROWS - STEPS) * 16 :, :]
        down_ref[b] = main_ref[b, : STEPS * 16, :]


def pack_noise(n_ref, out_ref, work, edges, *, groups, per):
    blocks = groups * per
    for b in range(blocks):
        for m in range(MEM):
            for l in range(LAYERS):
                for g in range(ROWS // SUB):
                    work[b, pl.ds(g * SUB * SUB + l * MEM + m, SUB, stride=SUB), :] = n_ref[
                        0, m, l, g * SUB : (g + 1) * SUB, b * BW : (b + 1) * BW
                    ]
    for d in range(groups):
        for h in range(2):
            def take(j):
                row = slice((h * SUB + j) * SUB, (h * SUB + j + 1) * SUB)
                return work[(d * per - 1) % blocks, row, :], work[(d * per + per) % blocks, row, :]

            edges[d, h * 16 : h * 16 + SUB, :] = halo_pack(take, SUB)
            edges[d, h * 16 + SUB : (h + 1) * 16, :] = jnp.zeros((SUB, BW), F32)
        for m in range(MEM):
            for c in range(per):
                for v in range(4):
                    out_ref[d, m, c * 4 + v] = work[d * per + c, pl.ds(v * 32 + m, SUB, stride=MEM), :]
            out_ref[d, m, per * 4] = edges[d, pl.ds(m, SUB, stride=MEM), :]


def clear_wall(buf, row, planes, edge):
    zero = jnp.zeros((STEPS * row, BW), F32)

    @pl.when(edge[0] == 0)
    def _():
        for b in range(planes):
            buf[b, : STEPS * row, :] = zero

    @pl.when(edge[0] == edge[1] - 1)
    def _():
        for b in range(planes):
            buf[b, (STEPS + ROWS) * row :, :] = zero


def row_range(edge, step):
    low = jnp.where(edge[0] == 0, STEPS, step + 1)
    high = jnp.where(edge[0] == edge[1] - 1, STEPS + ROWS, 2 * STEPS + ROWS - 1 - step)
    return low, high


def advance_members(edge, main_ref, up_ref, down_ref, out_ref, first, second, edges, *, groups, per):
    blocks = groups * per
    row = 2 * SUB
    for b in range(blocks):
        first[b, : STEPS * row, :] = up_ref[b]
        first[b, STEPS * row : (STEPS + ROWS) * row, :] = main_ref[b]
        first[b, (STEPS + ROWS) * row :, :] = down_ref[b]
    clear_wall(second, row, blocks, edge)
    drag = jnp.where(lax.broadcasted_iota(jnp.int32, (SUB, BW), 0) >= MEM, DRAG_STEP, 0.0).astype(F32)
    src, dst = first, second
    for step in range(STEPS):
        def body(i, _, src=src, dst=dst):
            def at(f, di):
                return pl.ds(pl.multiple_of((i + di) * row + f * SUB, SUB), SUB)

            def emit(b, q_new, psi_new):
                dst[b, at(0, 0), :] = q_new
                dst[b, at(1, 0), :] = psi_new

            ring_row(
                blocks,
                lambda f, b, di: src[b, at(f, di), :],
                lambda b, psi: pltpu.roll(psi, MEM, axis=0),
                emit,
                drag,
            )
            return 0

        low, high = row_range(edge, step)
        lax.fori_loop(low, high, body, 0)
        src, dst = dst, src
    base = STEPS * row
    for d in range(groups):
        for h in range(2):
            for f in range(2):
                def take(j):
                    s = base + (h * SUB + j) * row + f * SUB
                    rows = slice(s, s + SUB)
                    return src[(d * per - 1) % blocks, rows, :], src[(d * per + per) % blocks, rows, :]

                edges[d, (h * 2 + f) * SUB : (h * 2 + f + 1) * SUB, :] = halo_pack(take, SUB)
        for m in range(MEM):
            for c in range(per):
                for v in range(8):
                    out_ref[d, m, c * 8 + v] = src[
                        d * per + c, pl.ds(base + v * 32 + m, SUB, stride=MEM), :
                    ]
            out_ref[d, m, per * 8] = edges[d, pl.ds(m, SUB, stride=MEM), :]


def resample(
    parent, x_ref, n_ref, main_ref, edge_ref, up_ref, down_ref, z_ref, noise, *, members, per
):
    size = per * 8 + 1
    row = 4 * members

    def one(k, _):
        p = parent[k]
        for c in range(per):
            for v in range(8):
                main_ref[c, pl.ds(v * 8 * members + k, SUB, stride=members), :] = x_ref[
                    p, (c * 8 + v) * SUB : (c * 8 + v + 1) * SUB, :
                ]
            for v in range(4):
                noise[c, pl.ds(v * 8 * members + k, SUB, stride=members), :] = n_ref[k, c * 4 + v]
            for g in range(2):
                s = c * 64 + g * 32 + 2
                z_ref[c, pl.ds(g * SUB * members + k, SUB, stride=members), :] = x_ref[
                    k, pl.ds(s, SUB, stride=4), :
                ]
        edge_ref[pl.ds(k, SUB, stride=members), :] = (
            x_ref[p, size * SUB - SUB :, :] + n_ref[k, per * 4]
        )
        return 0

    lax.fori_loop(0, members, one, 0)
    for c in range(per):
        for r in range(ROWS):
            s = slice(r * row, r * row + 2 * members)
            main_ref[c, s, :] = main_ref[c, s, :] + noise[c, r * 2 * members : (r + 1) * 2 * members, :]
        for r in range(STEPS):
            up_ref[c * STEPS + r] = main_ref[c, (ROWS - STEPS + r) * row : (ROWS - STEPS + r + 1) * row, :]
            down_ref[c * STEPS + r] = main_ref[c, r * row : (r + 1) * row, :]
    up_ref[per * STEPS] = edge_ref[row:, :]
    down_ref[per * STEPS] = edge_ref[:row, :]


def advance_columns(
    edge, parent, main_ref, edge_ref, up_ref, down_ref, out_ref, z_ref, first, second, *, members, per
):
    row = 4 * members
    top = (STEPS + ROWS) * row
    for c in range(per):
        for r in range(STEPS):
            first[c, r * row : (r + 1) * row, :] = up_ref[c * STEPS + r]
            first[c, top + r * row : top + (r + 1) * row, :] = down_ref[c * STEPS + r]
        first[c, STEPS * row : top, :] = main_ref[c]
    for j in range(SUB):
        for h in range(2):
            s = (STEPS + h * SUB + j) * row
            first[per, s : s + row, :] = lane_roll(edge_ref[h * row : (h + 1) * row, :], -SEG * j)
        if j >= SUB - STEPS:
            s = (j - (SUB - STEPS)) * row
            first[per, s : s + row, :] = lane_roll(up_ref[per * STEPS], -SEG * j)
        if j < STEPS:
            s = top + j * row
            first[per, s : s + row, :] = lane_roll(down_ref[per * STEPS], -SEG * j)
    clear_wall(second, row, per + 1, edge)
    src, dst = first, second
    for step in range(STEPS):
        def body(i, _, src=src, dst=dst):
            for g in range(members // SUB):
                for l in range(LAYERS):
                    def at(f, layer, di):
                        s = (i + di) * row + (f * 2 + layer) * members + g * SUB
                        return pl.ds(pl.multiple_of(s, SUB), SUB)

                    def emit(b, q_new, psi_new):
                        dst[b, at(0, l, 0), :] = q_new
                        dst[b, at(1, l, 0), :] = psi_new

                    ring_row(
                        per + 1,
                        lambda f, b, di: src[b, at(f, l, di), :],
                        lambda b, psi: src[b, at(1, 1 - l, 0), :],
                        emit,
                        DRAG_STEP if l == 1 else None,
                    )
            return 0

        low, high = row_range(edge, step)
        lax.fori_loop(low, high, body, 0)
        src, dst = dst, src

    def one(k, _):
        p = parent[k]
        for c in range(per):
            for v in range(8):
                out_ref[k, c * 8 + v] = src[
                    c, pl.ds(STEPS * row + v * 8 * members + p, SUB, stride=members), :
                ]
        return 0

    lax.fori_loop(0, members, one, 0)
    for c in range(per):
        for r in range(ROWS):
            s = (STEPS + r) * row + 2 * members
            z_ref[c, r * members : (r + 1) * members, :] = src[c, s : s + members, :]


def unpack_state(y_ref, q_ref, p_ref, *, per):
    for c in range(per):
        for m in range(MEM):
            for l in range(LAYERS):
                for g in range(ROWS // SUB):
                    rows, cols = slice(g * SUB, (g + 1) * SUB), slice(c * BW, (c + 1) * BW)
                    s = c * 64 + g * 32 + l
                    q_ref[m, l, rows, cols] = y_ref[0, m, pl.ds(s, SUB, stride=4), :]
                    p_ref[m, l, rows, cols] = y_ref[0, m, pl.ds(s + 2, SUB, stride=4), :]


def score(rows_ref, z_ref, f_ref, o_ref, w_ref, out_ref, patch, total, *, members, per, chunk):
    a, c, j = pl.program_id(0), pl.program_id(1), pl.program_id(2)

    @pl.when((a == 0) & (c == 0) & (j == 0))
    def _():
        total[...] = jnp.zeros_like(total)

    @pl.when(j == 0)
    def _():
        start = rows_ref[a, c]
        for r in range(BR):
            s = pl.multiple_of((start + r) * members, SUB)
            part = z_ref[c, pl.ds(s, members), :]
            high = part.astype(jnp.bfloat16)
            patch[:members, r * BW : (r + 1) * BW] = high
            patch[members:, r * BW : (r + 1) * BW] = (part - high.astype(F32)).astype(jnp.bfloat16)

    weights = f_ref[0, 0]
    high = weights.astype(jnp.bfloat16)
    low = (weights - high.astype(F32)).astype(jnp.bfloat16)
    dims = (((1,), (1,)), ((), ()))
    main = lax.dot_general(patch[...], high, dims, preferred_element_type=F32)
    rest = lax.dot_general(patch[:members, :], low, dims, preferred_element_type=F32)
    predicted = main[:members] + (main[members:] + rest)
    miss = o_ref[0, 0] - predicted
    total[...] += w_ref[0, 0] * miss * miss

    @pl.when((a == pl.num_programs(0) - 1) & (c == pl.num_programs(1) - 1) & (j == pl.num_programs(2) - 1))
    def _():
        ones = jnp.full((SUB, total.shape[1]), -0.5, F32)
        out_ref[...] = lax.dot_general(
            ones, total[...], dims, precision=lax.Precision.HIGHEST, preferred_element_type=F32
        )


def shape(*dims):
    return jax.ShapeDtypeStruct(dims, F32)


def call(kernel, outs, scratch=(), scalars=0, name=None):
    def run(*args):
        specs = [pl.BlockSpec(memory_space=pltpu.SMEM)] * scalars
        specs += [pl.BlockSpec(memory_space=pltpu.VMEM)] * (len(args) - scalars)
        return pl.pallas_call(
            kernel,
            out_shape=outs,
            in_specs=specs,
            out_specs=[pl.BlockSpec(memory_space=pltpu.VMEM)] * len(outs),
            scratch_shapes=list(scratch),
            compiler_params=pltpu.CompilerParams(vmem_limit_bytes=VMEM_LIMIT),
            name=name,
        )(*args)

    return run


def shards(
    vorticity, streamfunction, model_noise, offspring, footprint, observed, precision, block_rows
):
    groups, tiles = lax.axis_size("dom"), lax.axis_size("tile")
    members = offspring.shape[1]
    width = vorticity.shape[3]
    blocks = width // BW
    per = blocks // groups
    bands, observations, cells = footprint.shape[0], footprint.shape[2], footprint.shape[3]

    running = jnp.cumsum(offspring, axis=1)
    slots = jnp.arange(members, dtype=jnp.int32)
    parent = jnp.sum((running[:, None, :] <= slots[None, :, None]).astype(jnp.int32), axis=2)
    parent = jnp.minimum(parent, members - 1)
    edge = jnp.stack([lax.axis_index("tile"), jnp.int32(tiles)]).astype(jnp.int32)

    up = [(i, i + 1) for i in range(tiles - 1)]
    down = [(i + 1, i) for i in range(tiles - 1)]

    fields = (MEM, LAYERS, ROWS)
    step_blocks = blocks // 4
    main, to_up, to_down = pl.pallas_call(
        functools.partial(pack_state, blocks=step_blocks),
        grid=(4,),
        in_specs=[
            pl.BlockSpec(fields + (step_blocks * BW,), lambda i: (0, 0, 0, i)),
            pl.BlockSpec(fields + (step_blocks * BW,), lambda i: (0, 0, 0, i)),
            pl.BlockSpec((1,) + fields + (step_blocks * BW,), lambda i: (0, 0, 0, 0, i)),
        ],
        out_specs=[
            pl.BlockSpec((step_blocks, ROWS * 16, BW), lambda i: (i, 0, 0)),
            pl.BlockSpec((step_blocks, STEPS * 16, BW), lambda i: (i, 0, 0)),
            pl.BlockSpec((step_blocks, STEPS * 16, BW), lambda i: (i, 0, 0)),
        ],
        out_shape=[
            shape(blocks, ROWS * 16, BW),
            shape(blocks, STEPS * 16, BW),
            shape(blocks, STEPS * 16, BW),
        ],
        name="pack_state",
    )(vorticity, streamfunction, model_noise)

    later_noise, to_up, to_down = lax.optimization_barrier((model_noise, to_up, to_down))
    from_below = lax.ppermute(to_up, "tile", up)
    from_above = lax.ppermute(to_down, "tile", down)

    noise = pl.pallas_call(
        functools.partial(pack_noise, groups=groups, per=per),
        grid=(1,),
        in_specs=[pl.BlockSpec((1,) + fields + (width,), lambda i: (1, 0, 0, 0, 0))],
        out_specs=pl.BlockSpec((groups, MEM, per * 4 + 1, SUB, BW), lambda i: (0, 0, 0, 0, 0)),
        out_shape=shape(groups, MEM, per * 4 + 1, SUB, BW),
        scratch_shapes=[pltpu.VMEM((blocks, ROWS * SUB, BW), F32), pltpu.VMEM((groups, 32, BW), F32)],
        name="pack_noise",
    )(later_noise)
    noise, main = lax.optimization_barrier((noise, main))
    noise = lax.all_to_all(noise, "dom", split_axis=0, concat_axis=0, tiled=True)
    noise = noise.reshape(members, per * 4 + 1, SUB, BW)

    work = (blocks, (ROWS + 2 * STEPS) * 16, BW)
    (sent,) = call(
        functools.partial(advance_members, groups=groups, per=per),
        [shape(groups, MEM, per * 8 + 1, SUB, BW)],
        [pltpu.VMEM(work, F32), pltpu.VMEM(work, F32), pltpu.VMEM((groups, 32, BW), F32)],
        scalars=1,
        name="advance_members",
    )(edge, main, from_below, from_above)
    owned = lax.all_to_all(sent, "dom", split_axis=0, concat_axis=0, tiled=True)
    owned = owned.reshape(members, (per * 8 + 1) * SUB, BW)

    row = 4 * members
    main, sides, to_up, to_down, surface = call(
        functools.partial(resample, members=members, per=per),
        [
            shape(per, ROWS * row, BW),
            shape(2 * row, BW),
            shape(per * STEPS + 1, row, BW),
            shape(per * STEPS + 1, row, BW),
            shape(per, ROWS * members, BW),
        ],
        [pltpu.VMEM((per, ROWS * 2 * members, BW), F32)],
        scalars=1,
        name="resample",
    )(parent[0], owned, noise)
    from_below = lax.ppermute(to_up, "tile", up)
    from_above = lax.ppermute(to_down, "tile", down)

    def likelihood(surface):
        chunk = 512
        obs = (bands, per, 1, observations)
        out = pl.pallas_call(
            functools.partial(score, members=members, per=per, chunk=chunk),
            grid=(bands, per, observations // chunk),
            in_specs=[
                pl.BlockSpec(memory_space=pltpu.SMEM),
                pl.BlockSpec((per, ROWS * members, BW), lambda a, c, j: (0, 0, 0)),
                pl.BlockSpec((1, 1, chunk, cells), lambda a, c, j: (a, c, j, 0)),
                pl.BlockSpec((1, 1, 1, chunk), lambda a, c, j: (a, c, 0, j)),
                pl.BlockSpec((1, 1, 1, chunk), lambda a, c, j: (a, c, 0, j)),
            ],
            out_specs=pl.BlockSpec((SUB, members), lambda a, c, j: (0, 0)),
            out_shape=shape(SUB, members),
            scratch_shapes=[
                pltpu.VMEM((2 * members, cells), jnp.bfloat16),
                pltpu.VMEM((members, chunk), F32),
            ],
            compiler_params=pltpu.CompilerParams(vmem_limit_bytes=VMEM_LIMIT),
            name="score",
        )(block_rows, surface, footprint, observed.reshape(obs), precision.reshape(obs))
        return out[:1]

    logs = [likelihood(surface)]
    main, logs[0] = lax.optimization_barrier((main, logs[0]))

    work = (per + 1, (ROWS + 2 * STEPS) * row, BW)
    back, surface = call(
        functools.partial(advance_columns, members=members, per=per),
        [shape(members, per * 8, SUB, BW), shape(per, ROWS * members, BW)],
        [pltpu.VMEM(work, F32), pltpu.VMEM(work, F32)],
        scalars=2,
        name="advance_columns",
    )(edge, parent[1], main, sides, from_below, from_above)
    back = back.reshape(groups, MEM, per * 64, BW)
    mine = lax.all_to_all(back, "dom", split_axis=0, concat_axis=0, tiled=True)
    logs.append(likelihood(surface))

    q_out, psi_out = pl.pallas_call(
        functools.partial(unpack_state, per=per),
        grid=(groups,),
        in_specs=[pl.BlockSpec((1, MEM, per * 64, BW), lambda i: (i, 0, 0, 0))],
        out_specs=[pl.BlockSpec(fields + (per * BW,), lambda i: (0, 0, 0, i))] * 2,
        out_shape=[shape(*fields, width)] * 2,
        name="unpack_state",
    )(mine)

    loglik = jnp.concatenate(logs, axis=0)
    for axis, size in (("dom", groups), ("tile", tiles)):
        hop = 1
        while hop < size:
            pairs = [(i, i ^ hop) for i in range(size)]
            loglik = loglik + lax.ppermute(loglik, axis, pairs)
            hop *= 2
    total_obs = observed.size * groups * tiles
    mean_loglik = loglik / total_obs
    highest = jnp.max(loglik, axis=1, keepdims=True)
    scaled = jnp.exp(loglik - highest)
    weights = scaled / jnp.sum(scaled, axis=1, keepdims=True)
    return (q_out, psi_out, mean_loglik, weights)


def solution(mesh):
    return jax.shard_map(
        shards,
        mesh=mesh,
        in_specs=(
            P("dom", None, "tile", None),
            P("dom", None, "tile", None),
            P(None, "dom", None, "tile", None),
            P(),
            P("tile", "dom", None, None),
            P("tile", "dom", None),
            P("tile", "dom", None),
            P("tile", "dom"),
        ),
        out_specs=(P("dom", None, "tile", None), P("dom", None, "tile", None), P(), P()),
        check_vma=False,
    )
```

```python
import functools

import jax
import jax.numpy as jnp
from jax import lax
from jax.experimental import pallas as pl
from jax.experimental.pallas import tpu as pltpu
from jax.sharding import PartitionSpec as P

STEPS = 6
CYCLES = 2
BW = 128
BR = 8
ROWS = 16
MEM = 4
LAYERS = 2
SUB = 8
SEG = 16
F32 = jnp.float32
VMEM_LIMIT = 56 * 1024 * 1024
DRAG_STEP = 0.1 * 0.2
HALF = 64
PARTS = 10
DEEP = ROWS + 2 * STEPS
FULL = 2 * HALF


def lanes():
    return lax.broadcasted_iota(jnp.int32, (SUB, BW), 1)


def lane_roll(x, shift):
    return pltpu.roll(x, shift % BW, axis=1)


def halo_pack(take):
    segment = ((lanes() + SEG // 2) // SEG) % SUB
    lower = lanes() < BW // 2
    packed = None
    for j in range(SUB):
        before, after = take(j)
        edge = lane_roll(jnp.where(lower, after, before), SEG * j)
        packed = edge if packed is None else jnp.where(segment == j, edge, packed)
    return packed


def wide_roll(x, shift):
    return pltpu.roll(x, shift % BW, axis=1)


def lower_half(rows):
    return lax.broadcasted_iota(jnp.int32, (rows, BW), 1) < HALF


def by_layer(turned):
    top, bottom = turned[:HALF], turned[HALF:]
    low = lower_half(HALF)
    return (
        jnp.where(low, top, wide_roll(bottom, HALF)),
        jnp.where(low, wide_roll(top, HALF), bottom),
    )


def to_layers(first, second):
    low = lower_half(HALF)
    top = jnp.where(low, first, wide_roll(second, HALF))
    bottom = jnp.where(low, wide_roll(first, HALF), second)
    return jnp.concatenate([top, bottom], axis=0)


def pack_field(*refs, blocks, noisy):
    x_ref, (main_ref, up_ref, down_ref, work) = refs[0], refs[-4:]
    g = pl.program_id(0)
    for b in range(blocks):
        cols = slice(b * BW, (b + 1) * BW)
        for m in range(MEM):
            for l in range(LAYERS):
                value = x_ref[m, l, :, cols]
                if noisy:
                    value = value + refs[1][0, m, l, :, cols]
                work[pl.ds(l * HALF + b * MEM + m, SUB, stride=FULL), :] = value
    for r in range(SUB):
        for l, part in enumerate(by_layer(work[r * FULL : (r + 1) * FULL, :].T)):
            main_ref[(r * 2 + l) * HALF : (r * 2 + l + 1) * HALF, :] = part

    @pl.when(g == 0)
    def _():
        down_ref[...] = main_ref[: STEPS * FULL, :]

    @pl.when(g == 1)
    def _():
        up_ref[...] = main_ref[(SUB - STEPS) * FULL :, :]


def pack_noise(n_ref, out_ref, work, wide, *, groups, per):
    blocks = groups * per
    for b in range(blocks):
        for m in range(MEM):
            for l in range(LAYERS):
                for g in range(ROWS // SUB):
                    value = n_ref[0, m, l, g * SUB : (g + 1) * SUB, b * BW : (b + 1) * BW]
                    s = l * HALF + b * MEM + m
                    work[pl.ds(g * SUB * FULL + s, SUB, stride=FULL), :] = value
                    wide[pl.ds(g * SUB * 2 * FULL + s, SUB, stride=2 * FULL), :] = value
    for r in range(ROWS):
        wide[(2 * r + 1) * FULL : (2 * r + 2) * FULL, :] = jnp.zeros((FULL, BW), F32)
    for d in range(groups):
        for m in range(MEM):
            def take(v):
                before = (d * per - 1) % blocks * MEM + m
                after = (d * per + per) % blocks * MEM + m
                return tuple(
                    wide[pl.ds(v * 4 * FULL + s, SUB, stride=HALF), :] for s in (before, after)
                )

            for c in range(per):
                for v in range(4):
                    s = v * 4 * FULL + (d * per + c) * MEM + m
                    out_ref[d, m, c * 4 + v] = work[pl.ds(s, SUB, stride=HALF), :]
            out_ref[d, m, per * 4] = halo_pack(take)


def place(natural, slot, dst, plane, body, left, right):
    natural[slot, :SUB, :] = left
    natural[slot, SUB : SUB + HALF, :] = body
    natural[slot, SUB + HALF :, :] = right
    for j in range(PARTS):
        dst[plane, j * SUB : (j + 1) * SUB, :] = natural[slot, pl.ds(j, SUB, stride=PARTS), :]


def margins(body, unit, left_end, right_end):
    lane = lanes()
    first, last = body[:SUB], body[HALF - SUB :]
    left = jnp.where(lane < HALF, wide_roll(last, HALF + unit), wide_roll(last, HALF))
    right = jnp.where(lane < HALF, wide_roll(first, HALF), wide_roll(first, HALF - unit))
    return jnp.where(lane < unit, left_end, left), jnp.where(lane >= BW - unit, right_end, right)


def run_steps(edge, first, second):
    zero = jnp.zeros((STEPS * 4, PARTS * SUB, BW), F32)

    @pl.when(edge[0] == 0)
    def _():
        second[: STEPS * 4] = zero

    @pl.when(edge[0] == edge[1] - 1)
    def _():
        second[(STEPS + ROWS) * 4 :] = zero

    src, dst = first, second
    for step in range(STEPS):
        low = jnp.where(edge[0] == 0, STEPS, step + 1)
        high = jnp.where(edge[0] == edge[1] - 1, STEPS + ROWS, DEEP - 1 - step)

        def body(i, _, src=src, dst=dst):
            for l in range(LAYERS):
                def load(f, j, di=0, layer=l):
                    return src[((i + di) * 2 + layer) * 2 + f, j * SUB : (j + 1) * SUB, :]

                west = tuple(pltpu.roll(load(f, PARTS - 1), 1, axis=0) for f in range(2))
                final = tuple(pltpu.roll(load(f, 0), SUB - 1, axis=0) for f in range(2))
                here = (load(0, 0), load(1, 0))
                for j in range(PARTS):
                    east = (load(0, j + 1), load(1, j + 1)) if j + 1 < PARTS else final
                    q, psi = here
                    psi_n, psi_s = load(1, j, 1), load(1, j, -1)
                    around = (psi_n + psi_s) + (east[1] + west[1])
                    along = east[1] - west[1]
                    psi_new = (around + load(1, j, 0, 1 - l) - q) * 0.2
                    change = along * ((load(0, j, 1) - load(0, j, -1)) + 1.0) - (
                        psi_n - psi_s
                    ) * (east[0] - west[0])
                    q_new = q - 0.025 * change
                    if l == 1:
                        q_new = q_new - DRAG_STEP * (around - 4.0 * psi)
                    dst[(i * 2 + l) * 2, j * SUB : (j + 1) * SUB, :] = q_new
                    dst[(i * 2 + l) * 2 + 1, j * SUB : (j + 1) * SUB, :] = psi_new
                    west, here = here, east
            return 0

        lax.fori_loop(low, high, body, 0)
        src, dst = dst, src
    return src


def turn_back(src, natural, turned):
    def body(r, _):
        for f in range(2):
            parts = []
            for l in range(LAYERS):
                slot = f * 2 + l
                plane = ((r + STEPS) * 2 + l) * 2 + f
                for j in range(PARTS):
                    natural[slot, pl.ds(j, SUB, stride=PARTS), :] = src[
                        plane, j * SUB : (j + 1) * SUB, :
                    ]
                parts.append(natural[slot, SUB : SUB + HALF, :])
            s = pl.multiple_of((r * 2 + f) * FULL, FULL)
            turned[pl.ds(s, FULL), :] = to_layers(*parts).T
        return 0

    lax.fori_loop(0, ROWS, body, 0)


def advance_members(
    edge, q_main, p_main, q_up, p_up, q_down, p_down, out_ref, first, second, natural, turned, *, groups, per
):
    def fill(refs, count, start):
        def body(r, _):
            for f in range(2):
                for l in range(LAYERS):
                    s = pl.multiple_of((r * 2 + l) * HALF, HALF)
                    value = refs[f][pl.ds(s, HALF), :]
                    ends = wide_roll(value[HALF - SUB :], MEM), wide_roll(value[:SUB], -MEM)
                    plane = ((r + start) * 2 + l) * 2 + f
                    place(natural, f * 2 + l, first, plane, value, *margins(value, MEM, *ends))
            return 0

        lax.fori_loop(0, count, body, 0)

    fill((q_main, p_main), ROWS, STEPS)
    fill((q_up, p_up), STEPS, 0)
    fill((q_down, p_down), STEPS, STEPS + ROWS)
    src = run_steps(edge, first, second)
    turn_back(src, natural, turned)
    for m in range(MEM):
        for d in range(groups):
            for c in range(per):
                for v in range(8):
                    s = v * 4 * FULL + (d * per + c) * MEM + m
                    out_ref[d, m, c * 8 + v] = turned[pl.ds(s, SUB, stride=HALF), :]
        for d in range(groups):
            def take(v):
                return out_ref[(d - 1) % groups, m, per * 8 - 8 + v], out_ref[(d + 1) % groups, m, v]

            out_ref[d, m, per * 8] = halo_pack(take)


def resample(
    parent, x_ref, n_ref, main_ref, edge_ref, up_ref, down_ref, z_ref, work, noise, *, members, per
):
    def one(k, _):
        p = parent[k]
        for c in range(per):
            for v in range(8):
                s = v * 4 * FULL + c * members + k
                work[pl.ds(s, SUB, stride=HALF), :] = x_ref[p, (c * 8 + v) * SUB : (c * 8 + v + 1) * SUB, :]
            for v in range(4):
                s = v * 4 * FULL + c * members + k
                noise[pl.ds(s, SUB, stride=HALF), :] = n_ref[k, c * 4 + v]
            for g in range(2):
                s = c * 64 + g * 32 + 2
                z_ref[c, pl.ds(g * SUB * members + k, SUB, stride=members), :] = x_ref[
                    k, pl.ds(s, SUB, stride=4), :
                ]
        edge_ref[pl.ds(k, SUB, stride=members), :] = x_ref[p, per * 64 :, :] + n_ref[k, per * 4]
        return 0

    lax.fori_loop(0, members, one, 0)
    for r in range(ROWS):
        for f in range(2):
            value = work[(r * 2 + f) * FULL : (r * 2 + f + 1) * FULL, :]
            if f == 0:
                value = value + noise[r * FULL : (r + 1) * FULL, :]
            for l, part in enumerate(by_layer(value.T)):
                s = ((r * 2 + l) * 2 + f) * HALF
                main_ref[s : s + HALF, :] = part
                if r < STEPS:
                    down_ref[s : s + HALF, :] = part
                if r >= ROWS - STEPS:
                    s -= (ROWS - STEPS) * 4 * HALF
                    up_ref[s : s + HALF, :] = part
    count = 4 * members
    segment = ((lax.broadcasted_iota(jnp.int32, (count, BW), 1) + SEG // 2) // SEG) % SUB
    even, odd = edge_ref[:count, :], wide_roll(edge_ref[count:, :], HALF)
    top = STEPS * 4 * HALF
    up_ref[top:, :] = jnp.where(segment >= 5, even, odd)
    down_ref[top:, :] = jnp.where(segment <= 2, even, odd)


def advance_columns(
    edge, parent, main_ref, edge_ref, up_ref, down_ref, out_ref, z_ref,
    first, second, natural, turned, sides, *, members, per
):
    top = STEPS * 4 * HALF
    count = 8 * members // BW
    for i in range(count):
        sides[i] = edge_ref[i * BW : (i + 1) * BW, :].T
    for i in range(count // 2):
        sides[count + i] = up_ref[top + i * BW : top + (i + 1) * BW, :].T
        sides[count + count // 2 + i] = down_ref[top + i * BW : top + (i + 1) * BW, :].T

    def put(source, at, plane, f, l, base, group):
        value = source[pl.ds(pl.multiple_of(at, HALF), HALF), :]
        index = base * BW + (f * 2 + l) * members
        matrix, offset = index // BW, index % BW
        before = pl.multiple_of((group * SEG + BW - SUB) % BW, SUB)
        after = pl.multiple_of(group * SEG, SUB)
        ends = (
            wide_roll(sides[matrix, pl.ds(before, SUB), :], -offset),
            wide_roll(sides[matrix, pl.ds(after, SUB), :], BW - members - offset),
        )
        place(natural, f * 2 + l, first, plane, value, *margins(value, members, *ends))

    def rows_own(v, _):
        for pair in range(2):
            for f in range(2):
                for l in range(LAYERS):
                    r = 2 * v + pair
                    at = ((r * 2 + l) * 2 + f) * HALF
                    put(main_ref, at, ((r + STEPS) * 2 + l) * 2 + f, f, l, pair * count // 2, v)
        return 0

    lax.fori_loop(0, SUB, rows_own, 0)

    def rows_beside(v, _):
        for pair in range(2):
            for f in range(2):
                for l in range(LAYERS):
                    r = 2 * v + pair
                    at = ((r * 2 + l) * 2 + f) * HALF
                    plane = (r * 2 + l) * 2 + f
                    put(up_ref, at, plane, f, l, count, v + 5 if pair == 0 else v + 1)
                    plane = ((r + STEPS + ROWS) * 2 + l) * 2 + f
                    put(down_ref, at, plane, f, l, count + count // 2, v if pair == 0 else v + 4)
        return 0

    lax.fori_loop(0, STEPS // 2, rows_beside, 0)
    src = run_steps(edge, first, second)
    turn_back(src, natural, turned)

    def one(k, _):
        p = parent[k]
        for c in range(per):
            for v in range(8):
                s = v * 4 * FULL + c * members + p
                out_ref[k, c * 8 + v] = turned[pl.ds(s, SUB, stride=HALF), :]
        return 0

    lax.fori_loop(0, members, one, 0)
    for c in range(per):
        for r in range(ROWS):
            s = (2 * r + 1) * FULL + c * members
            z_ref[c, r * members : (r + 1) * members, :] = turned[s : s + members, :]


def unpack_state(y_ref, q_ref, p_ref, *, groups, per):
    for d in range(groups):
        for c in range(per):
            b = d * per + c
            for l in range(LAYERS):
                for g in range(ROWS // SUB):
                    rows, cols = slice(g * SUB, (g + 1) * SUB), slice(b * BW, (b + 1) * BW)
                    s = c * 64 + g * 32 + l
                    q_ref[0, l, rows, cols] = y_ref[d, 0, pl.ds(s, SUB, stride=4), :]
                    p_ref[0, l, rows, cols] = y_ref[d, 0, pl.ds(s + 2, SUB, stride=4), :]


def score(rows_ref, z_ref, f_ref, o_ref, w_ref, out_ref, patch, total, *, members, per, chunk):
    a, c, j = pl.program_id(0), pl.program_id(1), pl.program_id(2)

    @pl.when((a == 0) & (c == 0) & (j == 0))
    def _():
        total[...] = jnp.zeros_like(total)

    @pl.when(j == 0)
    def _():
        start = rows_ref[a, c]
        for r in range(BR):
            s = pl.multiple_of((start + r) * members, SUB)
            part = z_ref[c, pl.ds(s, members), :]
            high = part.astype(jnp.bfloat16)
            patch[:members, r * BW : (r + 1) * BW] = high
            patch[members:, r * BW : (r + 1) * BW] = (part - high.astype(F32)).astype(jnp.bfloat16)

    weights = f_ref[0, 0]
    high = weights.astype(jnp.bfloat16)
    low = (weights - high.astype(F32)).astype(jnp.bfloat16)
    dims = (((1,), (1,)), ((), ()))
    main = lax.dot_general(patch[...], high, dims, preferred_element_type=F32)
    rest = lax.dot_general(patch[:members, :], low, dims, preferred_element_type=F32)
    predicted = main[:members] + (main[members:] + rest)
    miss = o_ref[0, 0] - predicted
    total[...] += w_ref[0, 0] * miss * miss

    @pl.when((a == pl.num_programs(0) - 1) & (c == pl.num_programs(1) - 1) & (j == pl.num_programs(2) - 1))
    def _():
        ones = jnp.full((SUB, total.shape[1]), -0.5, F32)
        out_ref[...] = lax.dot_general(
            ones, total[...], dims, precision=lax.Precision.HIGHEST, preferred_element_type=F32
        )


def shape(*dims):
    return jax.ShapeDtypeStruct(dims, F32)


def call(kernel, outs, scratch=(), scalars=0, name=None):
    def run(*args):
        specs = [pl.BlockSpec(memory_space=pltpu.SMEM)] * scalars
        specs += [pl.BlockSpec(memory_space=pltpu.VMEM)] * (len(args) - scalars)
        return pl.pallas_call(
            kernel,
            out_shape=outs,
            in_specs=specs,
            out_specs=[pl.BlockSpec(memory_space=pltpu.VMEM)] * len(outs),
            scratch_shapes=list(scratch),
            compiler_params=pltpu.CompilerParams(vmem_limit_bytes=VMEM_LIMIT),
            name=name,
        )(*args)

    return run


def shards(
    vorticity, streamfunction, model_noise, offspring, footprint, observed, precision, block_rows
):
    groups, tiles = lax.axis_size("dom"), lax.axis_size("tile")
    members = offspring.shape[1]
    width = vorticity.shape[3]
    blocks = width // BW
    per = blocks // groups
    bands, observations, cells = footprint.shape[0], footprint.shape[2], footprint.shape[3]

    running = jnp.cumsum(offspring, axis=1)
    slots = jnp.arange(members, dtype=jnp.int32)
    parent = jnp.sum((running[:, None, :] <= slots[None, :, None]).astype(jnp.int32), axis=2)
    parent = jnp.minimum(parent, members - 1)
    edge = jnp.stack([lax.axis_index("tile"), jnp.int32(tiles)]).astype(jnp.int32)

    up = [(i, i + 1) for i in range(tiles - 1)]
    down = [(i + 1, i) for i in range(tiles - 1)]
    params = pltpu.CompilerParams(vmem_limit_bytes=VMEM_LIMIT)

    def pack(field, *noise):
        half = (MEM, LAYERS, SUB, width)
        return pl.pallas_call(
            functools.partial(pack_field, blocks=blocks, noisy=bool(noise)),
            grid=(2,),
            in_specs=[pl.BlockSpec(half, lambda i: (0, 0, i, 0))]
            + [pl.BlockSpec((1,) + half, lambda i: (0, 0, 0, i, 0))] * len(noise),
            out_specs=[
                pl.BlockSpec((SUB * FULL, BW), lambda i: (i, 0)),
                pl.BlockSpec((STEPS * FULL, BW), lambda i: (0, 0)),
                pl.BlockSpec((STEPS * FULL, BW), lambda i: (0, 0)),
            ],
            out_shape=[shape(ROWS * FULL, BW), shape(STEPS * FULL, BW), shape(STEPS * FULL, BW)],
            scratch_shapes=[pltpu.VMEM((SUB * FULL, BW), F32)],
            compiler_params=params,
            name="pack_q" if noise else "pack_psi",
        )(field, *noise)

    p_main, p_up, p_down = pack(streamfunction)
    vorticity, p_up, p_down = lax.optimization_barrier((vorticity, p_up, p_down))
    p_below = lax.ppermute(p_up, "tile", up)
    p_above = lax.ppermute(p_down, "tile", down)
    q_main, q_up, q_down = pack(vorticity, model_noise)
    q_below = lax.ppermute(q_up, "tile", up)
    q_above = lax.ppermute(q_down, "tile", down)

    later_noise, p_below, p_above = lax.optimization_barrier((model_noise, p_below, p_above))
    noise = pl.pallas_call(
        functools.partial(pack_noise, groups=groups, per=per),
        grid=(1,),
        in_specs=[pl.BlockSpec((1, MEM, LAYERS, ROWS, width), lambda i: (1, 0, 0, 0, 0))],
        out_specs=pl.BlockSpec((groups, MEM, per * 4 + 1, SUB, BW), lambda i: (0, 0, 0, 0, 0)),
        out_shape=shape(groups, MEM, per * 4 + 1, SUB, BW),
        scratch_shapes=[pltpu.VMEM((ROWS * FULL, BW), F32), pltpu.VMEM((2 * ROWS * FULL, BW), F32)],
        compiler_params=params,
        name="pack_noise",
    )(later_noise)
    noise, q_below, q_above = lax.optimization_barrier((noise, q_below, q_above))
    noise = lax.all_to_all(noise, "dom", split_axis=0, concat_axis=0, tiled=True)
    noise = noise.reshape(members, per * 4 + 1, SUB, BW)

    work = [
        pltpu.VMEM((DEEP * 4, PARTS * SUB, BW), F32),
        pltpu.VMEM((DEEP * 4, PARTS * SUB, BW), F32),
        pltpu.VMEM((4, PARTS * SUB, BW), F32),
        pltpu.VMEM((2 * ROWS * FULL, BW), F32),
    ]
    (sent,) = call(
        functools.partial(advance_members, groups=groups, per=per),
        [shape(groups, MEM, per * 8 + 1, SUB, BW)],
        work,
        scalars=1,
        name="advance_members",
    )(edge, q_main, p_main, q_below, p_below, q_above, p_above)
    owned = lax.all_to_all(sent, "dom", split_axis=0, concat_axis=0, tiled=True)
    owned = owned.reshape(members, (per * 8 + 1) * SUB, BW)

    beside = STEPS * 4 * HALF + 4 * members
    main, sides, to_up, to_down, surface = call(
        functools.partial(resample, members=members, per=per),
        [
            shape(ROWS * 4 * HALF, BW),
            shape(8 * members, BW),
            shape(beside, BW),
            shape(beside, BW),
            shape(per, ROWS * members, BW),
        ],
        [pltpu.VMEM((2 * ROWS * FULL, BW), F32), pltpu.VMEM((ROWS * FULL, BW), F32)],
        scalars=1,
        name="resample",
    )(parent[0], owned, noise)
    from_below = lax.ppermute(to_up, "tile", up)
    from_above = lax.ppermute(to_down, "tile", down)

    def likelihood(surface):
        chunk = observations
        obs = (bands, per, 1, observations)
        out = pl.pallas_call(
            functools.partial(score, members=members, per=per, chunk=chunk),
            grid=(bands, per, observations // chunk),
            in_specs=[
                pl.BlockSpec(memory_space=pltpu.SMEM),
                pl.BlockSpec((per, ROWS * members, BW), lambda a, c, j: (0, 0, 0)),
                pl.BlockSpec((1, 1, chunk, cells), lambda a, c, j: (a, c, j, 0)),
                pl.BlockSpec((1, 1, 1, chunk), lambda a, c, j: (a, c, 0, j)),
                pl.BlockSpec((1, 1, 1, chunk), lambda a, c, j: (a, c, 0, j)),
            ],
            out_specs=pl.BlockSpec((SUB, members), lambda a, c, j: (0, 0)),
            out_shape=shape(SUB, members),
            scratch_shapes=[
                pltpu.VMEM((2 * members, cells), jnp.bfloat16),
                pltpu.VMEM((members, chunk), F32),
            ],
            compiler_params=params,
            name="score",
        )(block_rows, surface, footprint, observed.reshape(obs), precision.reshape(obs))
        return out[:1]

    logs = [likelihood(surface)]
    main, logs[0] = lax.optimization_barrier((main, logs[0]))

    back, surface = call(
        functools.partial(advance_columns, members=members, per=per),
        [shape(members, per * 8, SUB, BW), shape(per, ROWS * members, BW)],
        work + [pltpu.VMEM((members // SUB * 2, BW, BW), F32)],
        scalars=2,
        name="advance_columns",
    )(edge, parent[1], main, sides, from_below, from_above)
    back = back.reshape(groups, MEM, per * 64, BW)
    mine = lax.all_to_all(back, "dom", split_axis=0, concat_axis=0, tiled=True)
    logs.append(likelihood(surface))

    q_out, psi_out = pl.pallas_call(
        functools.partial(unpack_state, groups=groups, per=per),
        grid=(MEM,),
        in_specs=[pl.BlockSpec((groups, 1, per * 64, BW), lambda i: (0, i, 0, 0))],
        out_specs=[pl.BlockSpec((1, LAYERS, ROWS, width), lambda i: (i, 0, 0, 0))] * 2,
        out_shape=[shape(MEM, LAYERS, ROWS, width)] * 2,
        compiler_params=params,
        name="unpack_state",
    )(mine)

    loglik = jnp.concatenate(logs, axis=0)
    for axis, size in (("tile", tiles), ("dom", groups)):
        hop = 1
        while hop < size:
            pairs = [(i, i ^ hop) for i in range(size)]
            loglik = loglik + lax.ppermute(loglik, axis, pairs)
            hop *= 2
    total_obs = observed.size * groups * tiles
    mean_loglik = loglik / total_obs
    highest = jnp.max(loglik, axis=1, keepdims=True)
    scaled = jnp.exp(loglik - highest)
    weights = scaled / jnp.sum(scaled, axis=1, keepdims=True)
    return (q_out, psi_out, mean_loglik, weights)


def solution(mesh):
    return jax.shard_map(
        shards,
        mesh=mesh,
        in_specs=(
            P("dom", None, "tile", None),
            P("dom", None, "tile", None),
            P(None, "dom", None, "tile", None),
            P(),
            P("tile", "dom", None, None),
            P("tile", "dom", None),
            P("tile", "dom", None),
            P("tile", "dom"),
        ),
        out_specs=(P("dom", None, "tile", None), P("dom", None, "tile", None), P(), P()),
        check_vma=False,
    )
```

```python
import functools

import jax
import jax.numpy as jnp
from jax import lax
from jax.experimental import pallas as pl
from jax.experimental.pallas import tpu as pltpu
from jax.sharding import PartitionSpec as P

STEPS = 6
CYCLES = 2
BW = 128
BR = 8
ROWS = 16
MEM = 4
LAYERS = 2
SUB = 8
SEG = 16
F32 = jnp.float32
VMEM_LIMIT = 56 * 1024 * 1024
DRAG_STEP = 0.1 * 0.2
HALF = 64
PARTS = 10
QUAD = ROWS // 4
DEEP = ROWS + 2 * STEPS
FULL = 2 * HALF


def lanes():
    return lax.broadcasted_iota(jnp.int32, (SUB, BW), 1)


def lane_roll(x, shift):
    return pltpu.roll(x, shift % BW, axis=1)


def halo_pack(take):
    segment = ((lanes() + SEG // 2) // SEG) % SUB
    lower = lanes() < BW // 2
    packed = None
    for j in range(QUAD):
        before, after = take(j)
        edge = lane_roll(jnp.where(lower, after, before), SEG * j)
        packed = edge if packed is None else jnp.where(segment == j, edge, packed)
    return packed


def wide_roll(x, shift):
    return pltpu.roll(x, shift % BW, axis=1)


def lower_half(rows):
    return lax.broadcasted_iota(jnp.int32, (rows, BW), 1) < HALF


def by_layer(turned):
    top, bottom = turned[:HALF], turned[HALF:]
    low = lower_half(HALF)
    return (
        jnp.where(low, top, wide_roll(bottom, HALF)),
        jnp.where(low, wide_roll(top, HALF), bottom),
    )


def to_layers(first, second):
    low = lower_half(HALF)
    top = jnp.where(low, first, wide_roll(second, HALF))
    bottom = jnp.where(low, wide_roll(first, HALF), second)
    return jnp.concatenate([top, bottom], axis=0)


def pack_field(*refs, blocks, noisy):
    x_ref, (main_ref, up_ref, down_ref, work) = refs[0], refs[-4:]
    g = pl.program_id(0)
    for b in range(blocks):
        cols = slice(b * BW, (b + 1) * BW)
        for m in range(MEM):
            for l in range(LAYERS):
                value = x_ref[m, l, :, cols]
                if noisy:
                    value = value + refs[1][0, m, l, :, cols]
                work[pl.ds(l * HALF + b * MEM + m, SUB, stride=FULL), :] = value
    for r in range(SUB):
        for l, part in enumerate(by_layer(work[r * FULL : (r + 1) * FULL, :].T)):
            main_ref[(r * 2 + l) * HALF : (r * 2 + l + 1) * HALF, :] = part

    @pl.when(g == 0)
    def _():
        down_ref[...] = main_ref[: STEPS * FULL, :]

    @pl.when(g == 1)
    def _():
        up_ref[...] = main_ref[(SUB - STEPS) * FULL :, :]


def send_rows(work, base, out_ref, groups, per):
    blocks = groups * per
    for m in range(MEM):
        for d in range(groups):
            def rows(block, v):
                s = base + v * 4 * FULL + block % blocks * MEM + m
                return work[pl.ds(s, SUB, stride=HALF), :]

            for c in range(per):
                for v in range(QUAD):
                    out_ref[d, m, c * QUAD + v] = rows(d * per + c, v)
            out_ref[d, m, per * QUAD] = halo_pack(
                lambda v: (rows(d * per - 1, v), rows(d * per + per, v))
            )


def pack_noise(n_ref, out_ref, work, *, groups, per):
    for b in range(groups * per):
        for m in range(MEM):
            for l in range(LAYERS):
                for g in range(ROWS // SUB):
                    s = g * SUB * FULL + l * HALF + b * MEM + m
                    work[pl.ds(s, SUB, stride=FULL), :] = n_ref[
                        0, m, l, g * SUB : (g + 1) * SUB, b * BW : (b + 1) * BW
                    ]
    send_rows(work, 0, out_ref, groups, per)


def place(natural, slot, dst, plane, body, left, right):
    natural[slot, :SUB, :] = left
    natural[slot, SUB : SUB + HALF, :] = body
    natural[slot, SUB + HALF :, :] = right
    for j in range(PARTS):
        dst[plane, j * SUB : (j + 1) * SUB, :] = natural[slot, pl.ds(j, SUB, stride=PARTS), :]


def margins(body, unit, left_end, right_end):
    lane = lanes()
    first, last = body[:SUB], body[HALF - SUB :]
    left = jnp.where(lane < HALF, wide_roll(last, HALF + unit), wide_roll(last, HALF))
    right = jnp.where(lane < HALF, wide_roll(first, HALF), wide_roll(first, HALF - unit))
    return jnp.where(lane < unit, left_end, left), jnp.where(lane >= BW - unit, right_end, right)


def run_steps(edge, first, second):
    zero = jnp.zeros((STEPS * 4, PARTS * SUB, BW), F32)

    @pl.when(edge[0] == 0)
    def _():
        second[: STEPS * 4] = zero

    @pl.when(edge[0] == edge[1] - 1)
    def _():
        second[(STEPS + ROWS) * 4 :] = zero

    src, dst = first, second
    for step in range(STEPS):
        low = jnp.where(edge[0] == 0, STEPS, step + 1)
        high = jnp.where(edge[0] == edge[1] - 1, STEPS + ROWS, DEEP - 1 - step)

        def body(i, _, src=src, dst=dst):
            for l in range(LAYERS):
                def load(f, j, di=0, layer=l):
                    return src[((i + di) * 2 + layer) * 2 + f, j * SUB : (j + 1) * SUB, :]

                west = tuple(pltpu.roll(load(f, PARTS - 1), 1, axis=0) for f in range(2))
                final = tuple(pltpu.roll(load(f, 0), SUB - 1, axis=0) for f in range(2))
                here = (load(0, 0), load(1, 0))
                for j in range(PARTS):
                    east = (load(0, j + 1), load(1, j + 1)) if j + 1 < PARTS else final
                    q, psi = here
                    psi_n, psi_s = load(1, j, 1), load(1, j, -1)
                    around = (psi_n + psi_s) + (east[1] + west[1])
                    along = east[1] - west[1]
                    psi_new = (around + load(1, j, 0, 1 - l) - q) * 0.2
                    change = along * ((load(0, j, 1) - load(0, j, -1)) + 1.0) - (
                        psi_n - psi_s
                    ) * (east[0] - west[0])
                    q_new = q - 0.025 * change
                    if l == 1:
                        q_new = q_new - DRAG_STEP * (around - 4.0 * psi)
                    dst[(i * 2 + l) * 2, j * SUB : (j + 1) * SUB, :] = q_new
                    dst[(i * 2 + l) * 2 + 1, j * SUB : (j + 1) * SUB, :] = psi_new
                    west, here = here, east
            return 0

        lax.fori_loop(low, high, body, 0)
        src, dst = dst, src
    return src


def turn_back(src, natural, turned):
    def body(r, _):
        for f in range(2):
            parts = []
            for l in range(LAYERS):
                slot = f * 2 + l
                plane = ((r + STEPS) * 2 + l) * 2 + f
                for j in range(PARTS):
                    natural[slot, pl.ds(j, SUB, stride=PARTS), :] = src[
                        plane, j * SUB : (j + 1) * SUB, :
                    ]
                parts.append(natural[slot, SUB : SUB + HALF, :])
            s = pl.multiple_of((f * ROWS + r) * FULL, FULL)
            turned[pl.ds(s, FULL), :] = to_layers(*parts).T
        return 0

    lax.fori_loop(0, ROWS, body, 0)


def advance_members(
    edge, q_main, p_main, q_up, p_up, q_down, p_down, q_out, p_out,
    first, second, natural, turned, *, groups, per
):
    def fill(refs, count, start):
        def body(r, _):
            for f in range(2):
                for l in range(LAYERS):
                    s = pl.multiple_of((r * 2 + l) * HALF, HALF)
                    value = refs[f][pl.ds(s, HALF), :]
                    ends = wide_roll(value[HALF - SUB :], MEM), wide_roll(value[:SUB], -MEM)
                    plane = ((r + start) * 2 + l) * 2 + f
                    place(natural, f * 2 + l, first, plane, value, *margins(value, MEM, *ends))
            return 0

        lax.fori_loop(0, count, body, 0)

    fill((q_main, p_main), ROWS, STEPS)
    fill((q_up, p_up), STEPS, 0)
    fill((q_down, p_down), STEPS, STEPS + ROWS)
    src = run_steps(edge, first, second)
    turn_back(src, natural, turned)
    send_rows(turned, 0, q_out, groups, per)
    send_rows(turned, ROWS * FULL, p_out, groups, per)


def resample(parent, x_ref, *refs, members, per, noisy):
    main_ref, edge_ref, up_ref, down_ref = refs[noisy : noisy + 4]
    work = refs[-1]

    def one(k, _):
        p = parent[k]
        beside = x_ref[p, per * 32 :, :]
        for c in range(per):
            for v in range(QUAD):
                value = x_ref[p, (c * QUAD + v) * SUB : (c * QUAD + v + 1) * SUB, :]
                if noisy:
                    value = value + refs[0][k, (c * QUAD + v) * SUB : (c * QUAD + v + 1) * SUB, :]
                work[pl.ds(v * 4 * FULL + c * members + k, SUB, stride=HALF), :] = value
            if not noisy:
                for g in range(2):
                    refs[-2][c, pl.ds(g * SUB * members + k, SUB, stride=members), :] = x_ref[
                        k, pl.ds(c * 32 + g * 16, SUB, stride=2), :
                    ]
        if noisy:
            beside = beside + refs[0][k, per * 32 :, :]
        edge_ref[pl.ds(k, SUB, stride=members), :] = beside
        return 0

    lax.fori_loop(0, members, one, 0)
    for r in range(ROWS):
        for l, part in enumerate(by_layer(work[r * FULL : (r + 1) * FULL, :].T)):
            s = (r * 2 + l) * HALF
            main_ref[s : s + HALF, :] = part
            if r < STEPS:
                down_ref[s : s + HALF, :] = part
            if r >= ROWS - STEPS:
                s -= (ROWS - STEPS) * 2 * HALF
                up_ref[s : s + HALF, :] = part
    count = 2 * members
    segment = ((lax.broadcasted_iota(jnp.int32, (count, BW), 1) + SEG // 2) // SEG) % SUB
    for ref, start in ((up_ref, ROWS - STEPS), (down_ref, 0)):
        sides = None
        for i in range(STEPS):
            v, q = divmod(start + i, 4)
            rows = wide_roll(edge_ref[q * count : (q + 1) * count, :], SEG * (i - v))
            sides = rows if sides is None else jnp.where(segment == i, rows, sides)
        ref[STEPS * 2 * HALF :, :] = sides


def advance_columns(
    edge, parent, q_main, p_main, q_edge, p_edge, q_up, p_up, q_down, p_down, out_ref, z_ref,
    first, second, natural, turned, sides, *, members, per
):
    top = STEPS * 2 * HALF
    own = 8 * members // BW
    beside = own // 2
    for f, ref in enumerate((q_edge, p_edge)):
        for i in range(own):
            sides[f * own + i] = ref[i * BW : (i + 1) * BW, :].T
    for n, refs in enumerate(((q_up, p_up), (q_down, p_down))):
        both = jnp.concatenate([refs[0][top:, :], refs[1][top:, :]], axis=0)
        for i in range(beside):
            sides[2 * own + n * beside + i] = both[i * BW : (i + 1) * BW, :].T

    def put(source, r, row, f, l, base, index, group):
        value = source[pl.ds(pl.multiple_of((r * 2 + l) * HALF, HALF), HALF), :]
        matrix, offset = base + index * members // BW, index * members % BW
        before = pl.multiple_of((group * SEG + BW - SUB) % BW, SUB)
        after = pl.multiple_of(group * SEG, SUB)
        ends = (
            wide_roll(sides[matrix, pl.ds(before, SUB), :], -offset),
            wide_roll(sides[matrix, pl.ds(after, SUB), :], BW - members - offset),
        )
        plane = (row * 2 + l) * 2 + f
        place(natural, f * 2 + l, first, plane, value, *margins(value, members, *ends))

    def rows_own(v, _):
        for q in range(4):
            for f, source in enumerate((q_main, p_main)):
                for l in range(LAYERS):
                    put(source, 4 * v + q, 4 * v + q + STEPS, f, l, f * own, q * 2 + l, v)
        return 0

    lax.fori_loop(0, QUAD, rows_own, 0)

    def rows_beside(i, _):
        for n, refs in enumerate(((q_up, p_up), (q_down, p_down))):
            for f in range(2):
                for l in range(LAYERS):
                    row = i + n * (STEPS + ROWS)
                    put(refs[f], i, row, f, l, 2 * own + n * beside, f * 2 + l, i)
        return 0

    lax.fori_loop(0, STEPS, rows_beside, 0)
    src = run_steps(edge, first, second)
    turn_back(src, natural, turned)

    def one(k, _):
        p = parent[k]
        for c in range(per):
            for f in range(2):
                for v in range(QUAD):
                    s = f * ROWS * FULL + v * 4 * FULL + c * members + p
                    out_ref[k, (c * 2 + f) * QUAD + v] = turned[pl.ds(s, SUB, stride=HALF), :]
        return 0

    lax.fori_loop(0, members, one, 0)
    for c in range(per):
        for r in range(ROWS):
            s = (ROWS + r) * FULL + c * members
            z_ref[c, r * members : (r + 1) * members, :] = turned[s : s + members, :]


def unpack_state(y_ref, q_ref, p_ref, *, groups, per):
    for d in range(groups):
        for c in range(per):
            b = d * per + c
            for l in range(LAYERS):
                for g in range(ROWS // SUB):
                    rows, cols = slice(g * SUB, (g + 1) * SUB), slice(b * BW, (b + 1) * BW)
                    s = c * 64 + g * 16 + l
                    q_ref[0, l, rows, cols] = y_ref[d, 0, pl.ds(s, SUB, stride=2), :]
                    p_ref[0, l, rows, cols] = y_ref[d, 0, pl.ds(s + 32, SUB, stride=2), :]


def score(rows_ref, z_ref, f_ref, o_ref, w_ref, out_ref, patch, total, *, members, per, chunk):
    a, c, j = pl.program_id(0), pl.program_id(1), pl.program_id(2)

    @pl.when((a == 0) & (c == 0) & (j == 0))
    def _():
        total[...] = jnp.zeros_like(total)

    @pl.when(j == 0)
    def _():
        start = rows_ref[a, c]
        for r in range(BR):
            s = pl.multiple_of((start + r) * members, SUB)
            part = z_ref[c, pl.ds(s, members), :]
            high = part.astype(jnp.bfloat16)
            patch[:members, r * BW : (r + 1) * BW] = high
            patch[members:, r * BW : (r + 1) * BW] = (part - high.astype(F32)).astype(jnp.bfloat16)

    weights = f_ref[0, 0]
    high = weights.astype(jnp.bfloat16)
    low = (weights - high.astype(F32)).astype(jnp.bfloat16)
    dims = (((1,), (1,)), ((), ()))
    main = lax.dot_general(patch[...], high, dims, preferred_element_type=F32)
    rest = lax.dot_general(patch[:members, :], low, dims, preferred_element_type=F32)
    predicted = main[:members] + (main[members:] + rest)
    miss = o_ref[0, 0] - predicted
    total[...] += w_ref[0, 0] * miss * miss

    @pl.when((a == pl.num_programs(0) - 1) & (c == pl.num_programs(1) - 1) & (j == pl.num_programs(2) - 1))
    def _():
        ones = jnp.full((SUB, total.shape[1]), -0.5, F32)
        out_ref[...] = lax.dot_general(
            ones, total[...], dims, precision=lax.Precision.HIGHEST, preferred_element_type=F32
        )


CHEAP = pl.CostEstimate(flops=1000, transcendentals=0, bytes_accessed=1000)


def shape(*dims):
    return jax.ShapeDtypeStruct(dims, F32)


def call(kernel, outs, scratch=(), scalars=0, resident=9, name=None):
    def run(*args):
        args = args[:scalars] + tuple(
            pltpu.with_memory_space_constraint(x, pltpu.VMEM) if i < resident else x
            for i, x in enumerate(args[scalars:])
        )
        specs = [pl.BlockSpec(memory_space=pltpu.SMEM)] * scalars
        specs += [pl.BlockSpec(memory_space=pltpu.VMEM)] * (len(args) - scalars)
        return pl.pallas_call(
            kernel,
            out_shape=outs,
            in_specs=specs,
            out_specs=[pl.BlockSpec(memory_space=pltpu.VMEM)] * len(outs),
            scratch_shapes=list(scratch),
            compiler_params=pltpu.CompilerParams(vmem_limit_bytes=VMEM_LIMIT),
            cost_estimate=CHEAP,
            name=name,
        )(*args)

    return run


def shards(
    vorticity, streamfunction, model_noise, offspring, footprint, observed, precision, block_rows
):
    groups, tiles = lax.axis_size("dom"), lax.axis_size("tile")
    members = offspring.shape[1]
    width = vorticity.shape[3]
    blocks = width // BW
    per = blocks // groups
    bands, observations, cells = footprint.shape[0], footprint.shape[2], footprint.shape[3]

    running = jnp.cumsum(offspring, axis=1)
    slots = jnp.arange(members, dtype=jnp.int32)
    parent = jnp.sum((running[:, None, :] <= slots[None, :, None]).astype(jnp.int32), axis=2)
    parent = jnp.minimum(parent, members - 1)
    edge = jnp.stack([lax.axis_index("tile"), jnp.int32(tiles)]).astype(jnp.int32)

    up = [(i, i + 1) for i in range(tiles - 1)]
    down = [(i + 1, i) for i in range(tiles - 1)]
    params = pltpu.CompilerParams(vmem_limit_bytes=VMEM_LIMIT)

    def pack(field, *noise):
        half = (MEM, LAYERS, SUB, width)
        return pl.pallas_call(
            functools.partial(pack_field, blocks=blocks, noisy=bool(noise)),
            grid=(2,),
            in_specs=[pl.BlockSpec(half, lambda i: (0, 0, i, 0))]
            + [pl.BlockSpec((1,) + half, lambda i: (0, 0, 0, i, 0))] * len(noise),
            out_specs=[
                pl.BlockSpec((SUB * FULL, BW), lambda i: (i, 0)),
                pl.BlockSpec((STEPS * FULL, BW), lambda i: (0, 0)),
                pl.BlockSpec((STEPS * FULL, BW), lambda i: (0, 0)),
            ],
            out_shape=[shape(ROWS * FULL, BW), shape(STEPS * FULL, BW), shape(STEPS * FULL, BW)],
            scratch_shapes=[pltpu.VMEM((SUB * FULL, BW), F32)],
            compiler_params=params,
            cost_estimate=CHEAP,
            name="pack_q" if noise else "pack_psi",
        )(field, *noise)

    p_main, p_up, p_down = pack(streamfunction)
    vorticity, p_up, p_down = lax.optimization_barrier((vorticity, p_up, p_down))
    p_below = lax.ppermute(p_up, "tile", up)
    p_above = lax.ppermute(p_down, "tile", down)
    q_main, q_up, q_down = pack(vorticity, model_noise)
    q_below = lax.ppermute(q_up, "tile", up)
    q_above = lax.ppermute(q_down, "tile", down)

    later_noise, p_below, p_above = lax.optimization_barrier((model_noise, p_below, p_above))
    noise = pl.pallas_call(
        functools.partial(pack_noise, groups=groups, per=per),
        grid=(1,),
        in_specs=[pl.BlockSpec((1, MEM, LAYERS, ROWS, width), lambda i: (1, 0, 0, 0, 0))],
        out_specs=pl.BlockSpec((groups, MEM, per * 4 + 1, SUB, BW), lambda i: (0, 0, 0, 0, 0)),
        out_shape=shape(groups, MEM, per * 4 + 1, SUB, BW),
        scratch_shapes=[pltpu.VMEM((ROWS * FULL, BW), F32)],
        compiler_params=params,
        cost_estimate=CHEAP,
        name="pack_noise",
    )(later_noise)
    noise, q_below, q_above = lax.optimization_barrier((noise, q_below, q_above))
    noise = lax.all_to_all(noise, "dom", split_axis=0, concat_axis=0, tiled=True)
    noise = noise.reshape(members, (per * 4 + 1) * SUB, BW)

    work = [
        pltpu.VMEM((DEEP * 4, PARTS * SUB, BW), F32),
        pltpu.VMEM((DEEP * 4, PARTS * SUB, BW), F32),
        pltpu.VMEM((4, PARTS * SUB, BW), F32),
        pltpu.VMEM((2 * ROWS * FULL, BW), F32),
    ]
    q_sent, p_sent = call(
        functools.partial(advance_members, groups=groups, per=per),
        [shape(groups, MEM, per * 4 + 1, SUB, BW)] * 2,
        work,
        scalars=1,
        resident=2,
        name="advance_members",
    )(edge, q_main, p_main, q_below, p_below, q_above, p_above)
    beside = STEPS * 2 * HALF + 2 * members
    pieces = [shape(ROWS * 2 * HALF, BW), shape(8 * members, BW), shape(beside, BW), shape(beside, BW)]

    def spread(sent):
        owned = lax.all_to_all(sent, "dom", split_axis=0, concat_axis=0, tiled=True)
        return owned.reshape(members, (per * 4 + 1) * SUB, BW)

    def exchange(owned, noise=()):
        extra = [] if noise else [shape(per, ROWS * members, BW)]
        main, edges, to_up, to_down, *surface = call(
            functools.partial(resample, members=members, per=per, noisy=len(noise)),
            pieces + extra,
            [pltpu.VMEM((ROWS * FULL, BW), F32)],
            scalars=1,
            name="resample_q" if noise else "resample_psi",
        )(parent[0], owned, *noise)
        below = lax.ppermute(to_up, "tile", up)
        above = lax.ppermute(to_down, "tile", down)
        return main, edges, below, above, *surface

    p_sent, noise = lax.optimization_barrier((p_sent, noise))
    p_owned = spread(p_sent)
    q_sent, p_owned = lax.optimization_barrier((q_sent, p_owned))
    q_owned = spread(q_sent)
    p_main, p_edge, p_below, p_above, surface = exchange(p_owned)
    q_main, q_edge, q_below, q_above = exchange(q_owned, (noise,))

    def likelihood(surface):
        chunk = observations
        obs = (bands, per, 1, observations)
        out = pl.pallas_call(
            functools.partial(score, members=members, per=per, chunk=chunk),
            grid=(bands, per, observations // chunk),
            in_specs=[
                pl.BlockSpec(memory_space=pltpu.SMEM),
                pl.BlockSpec((per, ROWS * members, BW), lambda a, c, j: (0, 0, 0)),
                pl.BlockSpec((1, 1, chunk, cells), lambda a, c, j: (a, c, j, 0)),
                pl.BlockSpec((1, 1, 1, chunk), lambda a, c, j: (a, c, 0, j)),
                pl.BlockSpec((1, 1, 1, chunk), lambda a, c, j: (a, c, 0, j)),
            ],
            out_specs=pl.BlockSpec((SUB, members), lambda a, c, j: (0, 0)),
            out_shape=shape(SUB, members),
            scratch_shapes=[
                pltpu.VMEM((2 * members, cells), jnp.bfloat16),
                pltpu.VMEM((members, chunk), F32),
            ],
            compiler_params=params,
            cost_estimate=CHEAP,
            name="score",
        )(block_rows, surface, footprint, observed.reshape(obs), precision.reshape(obs))
        return out[:1]

    logs = [likelihood(surface)]
    p_main, logs[0] = lax.optimization_barrier((p_main, logs[0]))

    back, surface = call(
        functools.partial(advance_columns, members=members, per=per),
        [shape(members, per * 8, SUB, BW), shape(per, ROWS * members, BW)],
        work + [pltpu.VMEM((members // SUB * 2, BW, BW), F32)],
        scalars=2,
        name="advance_columns",
    )(edge, parent[1], q_main, p_main, q_edge, p_edge, q_below, p_below, q_above, p_above)
    back = back.reshape(groups, MEM, per * 64, BW)
    mine = lax.all_to_all(back, "dom", split_axis=0, concat_axis=0, tiled=True)
    logs.append(likelihood(surface))

    q_out, psi_out = pl.pallas_call(
        functools.partial(unpack_state, groups=groups, per=per),
        grid=(MEM,),
        in_specs=[pl.BlockSpec((groups, 1, per * 64, BW), lambda i: (0, i, 0, 0))],
        out_specs=[pl.BlockSpec((1, LAYERS, ROWS, width), lambda i: (i, 0, 0, 0))] * 2,
        out_shape=[shape(MEM, LAYERS, ROWS, width)] * 2,
        compiler_params=params,
        cost_estimate=CHEAP,
        name="unpack_state",
    )(mine)

    loglik = jnp.concatenate(logs, axis=0)
    for axis, size in (("tile", tiles), ("dom", groups)):
        hop = 1
        while hop < size:
            pairs = [(i, i ^ hop) for i in range(size)]
            loglik = loglik + lax.ppermute(loglik, axis, pairs)
            hop *= 2
    total_obs = observed.size * groups * tiles
    mean_loglik = loglik / total_obs
    highest = jnp.max(loglik, axis=1, keepdims=True)
    scaled = jnp.exp(loglik - highest)
    weights = scaled / jnp.sum(scaled, axis=1, keepdims=True)
    return (q_out, psi_out, mean_loglik, weights)


def solution(mesh):
    return jax.shard_map(
        shards,
        mesh=mesh,
        in_specs=(
            P("dom", None, "tile", None),
            P("dom", None, "tile", None),
            P(None, "dom", None, "tile", None),
            P(),
            P("tile", "dom", None, None),
            P("tile", "dom", None),
            P("tile", "dom", None),
            P("tile", "dom"),
        ),
        out_specs=(P("dom", None, "tile", None), P("dom", None, "tile", None), P(), P()),
        check_vma=False,
    )
```

```python
import functools

import jax
import jax.numpy as jnp
from jax import lax
from jax.experimental import pallas as pl
from jax.experimental.pallas import tpu as pltpu
from jax.sharding import PartitionSpec as P

STEPS = 6
CYCLES = 2
BW = 128
BR = 8
ROWS = 16
MEM = 4
LAYERS = 2
SUB = 8
SEG = 16
F32 = jnp.float32
VMEM_LIMIT = 20 * 1024 * 1024
DRAG_STEP = 0.1 * 0.2
HALF = 64
PARTS = 10
QUAD = ROWS // 4
DEEP = ROWS + 2 * STEPS
FULL = 2 * HALF


def lanes():
    return lax.broadcasted_iota(jnp.int32, (SUB, BW), 1)


def lane_roll(x, shift):
    return pltpu.roll(x, shift % BW, axis=1)


def halo_pack(take):
    segment = ((lanes() + SEG // 2) // SEG) % SUB
    lower = lanes() < BW // 2
    packed = None
    for j in range(QUAD):
        before, after = take(j)
        edge = lane_roll(jnp.where(lower, after, before), SEG * j)
        packed = edge if packed is None else jnp.where(segment == j, edge, packed)
    return packed


def wide_roll(x, shift):
    return pltpu.roll(x, shift % BW, axis=1)


def lower_half(rows):
    return lax.broadcasted_iota(jnp.int32, (rows, BW), 1) < HALF


def by_layer(turned):
    top, bottom = turned[:HALF], turned[HALF:]
    low = lower_half(HALF)
    return (
        jnp.where(low, top, wide_roll(bottom, HALF)),
        jnp.where(low, wide_roll(top, HALF), bottom),
    )


def to_layers(first, second):
    low = lower_half(HALF)
    top = jnp.where(low, first, wide_roll(second, HALF))
    bottom = jnp.where(low, wide_roll(first, HALF), second)
    return jnp.concatenate([top, bottom], axis=0)


def pack_field(*refs, blocks, noisy):
    x_ref, (main_ref, up_ref, down_ref, work) = refs[0], refs[-4:]
    g = pl.program_id(0)
    for b in range(blocks):
        cols = slice(b * BW, (b + 1) * BW)
        for m in range(MEM):
            for l in range(LAYERS):
                value = x_ref[m, l, :, cols]
                if noisy:
                    value = value + refs[1][0, m, l, :, cols]
                work[pl.ds(l * HALF + b * MEM + m, SUB, stride=FULL), :] = value
    for r in range(SUB):
        for l, part in enumerate(by_layer(work[r * FULL : (r + 1) * FULL, :].T)):
            main_ref[(r * 2 + l) * HALF : (r * 2 + l + 1) * HALF, :] = part

    @pl.when(g == 0)
    def _():
        down_ref[...] = main_ref[: STEPS * FULL, :]

    @pl.when(g == 1)
    def _():
        up_ref[...] = main_ref[(SUB - STEPS) * FULL :, :]


def send_rows(work, base, out_ref, groups, per):
    blocks = groups * per
    for m in range(MEM):
        for d in range(groups):
            def rows(block, v):
                s = base + v * 4 * FULL + block % blocks * MEM + m
                return work[pl.ds(s, SUB, stride=HALF), :]

            for c in range(per):
                for v in range(QUAD):
                    out_ref[d, m, c * QUAD + v] = rows(d * per + c, v)
            out_ref[d, m, per * QUAD] = halo_pack(
                lambda v: (rows(d * per - 1, v), rows(d * per + per, v))
            )


def pack_noise(n_ref, out_ref, work, *, groups, per):
    for b in range(groups * per):
        for m in range(MEM):
            for l in range(LAYERS):
                for g in range(ROWS // SUB):
                    s = g * SUB * FULL + l * HALF + b * MEM + m
                    work[pl.ds(s, SUB, stride=FULL), :] = n_ref[
                        0, m, l, g * SUB : (g + 1) * SUB, b * BW : (b + 1) * BW
                    ]
    send_rows(work, 0, out_ref, groups, per)


def place(natural, slot, dst, plane, body, left, right):
    natural[slot, :SUB, :] = left
    natural[slot, SUB : SUB + HALF, :] = body
    natural[slot, SUB + HALF :, :] = right
    for j in range(PARTS):
        dst[plane, j * SUB : (j + 1) * SUB, :] = natural[slot, pl.ds(j, SUB, stride=PARTS), :]


def margins(body, unit, left_end, right_end):
    lane = lanes()
    first, last = body[:SUB], body[HALF - SUB :]
    left = jnp.where(lane < HALF, wide_roll(last, HALF + unit), wide_roll(last, HALF))
    right = jnp.where(lane < HALF, wide_roll(first, HALF), wide_roll(first, HALF - unit))
    return jnp.where(lane < unit, left_end, left), jnp.where(lane >= BW - unit, right_end, right)


def run_steps(edge, first, second):
    zero = jnp.zeros((STEPS * 4, PARTS * SUB, BW), F32)

    @pl.when(edge[0] == 0)
    def _():
        second[: STEPS * 4] = zero

    @pl.when(edge[0] == edge[1] - 1)
    def _():
        second[(STEPS + ROWS) * 4 :] = zero

    src, dst = first, second
    for step in range(STEPS):
        low = jnp.where(edge[0] == 0, STEPS, step + 1)
        high = jnp.where(edge[0] == edge[1] - 1, STEPS + ROWS, DEEP - 1 - step)

        def body(i, _, src=src, dst=dst):
            for l in range(LAYERS):
                def load(f, j, di=0, layer=l):
                    return src[((i + di) * 2 + layer) * 2 + f, j * SUB : (j + 1) * SUB, :]

                west = tuple(pltpu.roll(load(f, PARTS - 1), 1, axis=0) for f in range(2))
                final = tuple(pltpu.roll(load(f, 0), SUB - 1, axis=0) for f in range(2))
                here = (load(0, 0), load(1, 0))
                for j in range(PARTS):
                    east = (load(0, j + 1), load(1, j + 1)) if j + 1 < PARTS else final
                    q, psi = here
                    psi_n, psi_s = load(1, j, 1), load(1, j, -1)
                    around = (psi_n + psi_s) + (east[1] + west[1])
                    along = east[1] - west[1]
                    psi_new = (around + load(1, j, 0, 1 - l) - q) * 0.2
                    change = along * ((load(0, j, 1) - load(0, j, -1)) + 1.0) - (
                        psi_n - psi_s
                    ) * (east[0] - west[0])
                    q_new = q - 0.025 * change
                    if l == 1:
                        q_new = q_new - DRAG_STEP * (around - 4.0 * psi)
                    dst[(i * 2 + l) * 2, j * SUB : (j + 1) * SUB, :] = q_new
                    dst[(i * 2 + l) * 2 + 1, j * SUB : (j + 1) * SUB, :] = psi_new
                    west, here = here, east
            return 0

        lax.fori_loop(low, high, body, 0)
        src, dst = dst, src
    return src


def turn_back(src, natural, turned):
    def body(pair, _):
        for turn in range(4):
            r, f = 2 * pair + turn // 2, turn % 2
            parts = []
            for l in range(LAYERS):
                slot = turn * 2 + l
                plane = ((r + STEPS) * 2 + l) * 2 + f
                for j in range(PARTS):
                    natural[slot, pl.ds(j, SUB, stride=PARTS), :] = src[
                        plane, j * SUB : (j + 1) * SUB, :
                    ]
                parts.append(natural[slot, SUB : SUB + HALF, :])
            s = pl.multiple_of((f * ROWS + r) * FULL, FULL)
            turned[pl.ds(s, FULL), :] = to_layers(*parts).T
        return 0

    lax.fori_loop(0, ROWS // 2, body, 0)


def advance_members(
    edge, q_main, p_main, q_up, p_up, q_down, p_down, q_out, p_out,
    first, second, natural, turned, *, groups, per
):
    def fill(refs, count, start):
        def body(pair, _):
            for turn in range(4):
                r, f = 2 * pair + turn // 2, turn % 2
                for l in range(LAYERS):
                    s = pl.multiple_of((r * 2 + l) * HALF, HALF)
                    value = refs[f][pl.ds(s, HALF), :]
                    ends = wide_roll(value[HALF - SUB :], MEM), wide_roll(value[:SUB], -MEM)
                    plane = ((r + start) * 2 + l) * 2 + f
                    place(natural, turn * 2 + l, first, plane, value, *margins(value, MEM, *ends))
            return 0

        lax.fori_loop(0, count // 2, body, 0)

    fill((q_main, p_main), ROWS, STEPS)
    fill((q_up, p_up), STEPS, 0)
    fill((q_down, p_down), STEPS, STEPS + ROWS)
    src = run_steps(edge, first, second)
    turn_back(src, natural, turned)
    send_rows(turned, 0, q_out, groups, per)
    send_rows(turned, ROWS * FULL, p_out, groups, per)


def resample(parent, x_ref, *refs, members, per, noisy):
    main_ref, edge_ref, up_ref, down_ref = refs[noisy : noisy + 4]
    work = refs[-1]

    def one(k, _):
        p = parent[k]
        beside = x_ref[p, per * 32 :, :]
        for c in range(per):
            for v in range(QUAD):
                value = x_ref[p, (c * QUAD + v) * SUB : (c * QUAD + v + 1) * SUB, :]
                if noisy:
                    value = value + refs[0][k, (c * QUAD + v) * SUB : (c * QUAD + v + 1) * SUB, :]
                work[pl.ds(v * 4 * FULL + c * members + k, SUB, stride=HALF), :] = value
            if not noisy:
                for g in range(2):
                    refs[-2][c, pl.ds(g * SUB * members + k, SUB, stride=members), :] = x_ref[
                        k, pl.ds(c * 32 + g * 16, SUB, stride=2), :
                    ]
        if noisy:
            beside = beside + refs[0][k, per * 32 :, :]
        edge_ref[pl.ds(k, SUB, stride=members), :] = beside
        return 0

    lax.fori_loop(0, members, one, 0)
    for r in range(ROWS):
        for l, part in enumerate(by_layer(work[r * FULL : (r + 1) * FULL, :].T)):
            s = (r * 2 + l) * HALF
            main_ref[s : s + HALF, :] = part
            if r < STEPS:
                down_ref[s : s + HALF, :] = part
            if r >= ROWS - STEPS:
                s -= (ROWS - STEPS) * 2 * HALF
                up_ref[s : s + HALF, :] = part
    count = 2 * members
    segment = ((lax.broadcasted_iota(jnp.int32, (count, BW), 1) + SEG // 2) // SEG) % SUB
    for ref, start in ((up_ref, ROWS - STEPS), (down_ref, 0)):
        sides = None
        for i in range(STEPS):
            v, q = divmod(start + i, 4)
            rows = wide_roll(edge_ref[q * count : (q + 1) * count, :], SEG * (i - v))
            sides = rows if sides is None else jnp.where(segment == i, rows, sides)
        ref[STEPS * 2 * HALF :, :] = sides


def advance_columns(
    edge, parent, q_main, p_main, q_edge, p_edge, q_up, p_up, q_down, p_down, out_ref, z_ref,
    first, second, natural, turned, sides, *, members, per
):
    top = STEPS * 2 * HALF
    own = 8 * members // BW
    beside = own // 2
    for f, ref in enumerate((q_edge, p_edge)):
        for i in range(own):
            sides[f * own + i] = ref[i * BW : (i + 1) * BW, :].T
    for n, refs in enumerate(((q_up, p_up), (q_down, p_down))):
        both = jnp.concatenate([refs[0][top:, :], refs[1][top:, :]], axis=0)
        for i in range(beside):
            sides[2 * own + n * beside + i] = both[i * BW : (i + 1) * BW, :].T

    def put(source, r, row, f, l, base, index, group, turn):
        value = source[pl.ds(pl.multiple_of((r * 2 + l) * HALF, HALF), HALF), :]
        matrix, offset = base + index * members // BW, index * members % BW
        before = pl.multiple_of((group * SEG + BW - SUB) % BW, SUB)
        after = pl.multiple_of(group * SEG, SUB)
        ends = (
            wide_roll(sides[matrix, pl.ds(before, SUB), :], -offset),
            wide_roll(sides[matrix, pl.ds(after, SUB), :], BW - members - offset),
        )
        plane = (row * 2 + l) * 2 + f
        place(natural, turn * 4 + f * 2 + l, first, plane, value, *margins(value, members, *ends))

    def rows_own(v, _):
        for q in range(4):
            for f, source in enumerate((q_main, p_main)):
                for l in range(LAYERS):
                    put(source, 4 * v + q, 4 * v + q + STEPS, f, l, f * own, q * 2 + l, v, q % 2)
        return 0

    lax.fori_loop(0, QUAD, rows_own, 0)

    def rows_beside(i, _):
        for n, refs in enumerate(((q_up, p_up), (q_down, p_down))):
            for f in range(2):
                for l in range(LAYERS):
                    row = i + n * (STEPS + ROWS)
                    put(refs[f], i, row, f, l, 2 * own + n * beside, f * 2 + l, i, n)
        return 0

    lax.fori_loop(0, STEPS, rows_beside, 0)
    src = run_steps(edge, first, second)
    turn_back(src, natural, turned)

    def one(k, _):
        p = parent[k]
        for c in range(per):
            for f in range(2):
                for v in range(QUAD):
                    s = f * ROWS * FULL + v * 4 * FULL + c * members + p
                    out_ref[k, (c * 2 + f) * QUAD + v] = turned[pl.ds(s, SUB, stride=HALF), :]
        return 0

    lax.fori_loop(0, members, one, 0)
    for c in range(per):
        for r in range(ROWS):
            s = (ROWS + r) * FULL + c * members
            z_ref[c, r * members : (r + 1) * members, :] = turned[s : s + members, :]


def unpack_state(y_ref, q_ref, p_ref, *, groups, per):
    for d in range(groups):
        for c in range(per):
            b = d * per + c
            for m, l in [(m, l) for m in range(MEM) for l in range(LAYERS)]:
                for g in range(ROWS // SUB):
                    rows, cols = slice(g * SUB, (g + 1) * SUB), slice(b * BW, (b + 1) * BW)
                    s = c * 64 + g * 16 + l
                    q_ref[m, l, rows, cols] = y_ref[d, m, pl.ds(s, SUB, stride=2), :]
                    p_ref[m, l, rows, cols] = y_ref[d, m, pl.ds(s + 32, SUB, stride=2), :]


def score(rows_ref, z_ref, f_ref, o_ref, w_ref, first_ref, out_ref, patch, total, *, members, cycle):
    a, c = pl.program_id(0), pl.program_id(1)

    @pl.when((a == 0) & (c == 0))
    def _():
        total[...] = jnp.zeros_like(total)

    start = rows_ref[a, c]
    for r in range(BR):
        s = pl.multiple_of((start + r) * members, SUB)
        part = z_ref[c, pl.ds(s, members), :]
        high = part.astype(jnp.bfloat16)
        patch[:members, r * BW : (r + 1) * BW] = high
        patch[members:, r * BW : (r + 1) * BW] = (part - high.astype(F32)).astype(jnp.bfloat16)

    weights = f_ref[0, 0]
    high = weights.astype(jnp.bfloat16)
    low = (weights - high.astype(F32)).astype(jnp.bfloat16)
    dims = (((1,), (1,)), ((), ()))
    main = lax.dot_general(patch[...], high, dims, preferred_element_type=F32)
    rest = lax.dot_general(patch[:members, :], low, dims, preferred_element_type=F32)
    predicted = main[:members] + (main[members:] + rest)
    miss = o_ref[0, pl.ds(c, 1), :] - predicted
    total[...] += w_ref[0, pl.ds(c, 1), :] * miss * miss

    @pl.when((a == pl.num_programs(0) - 1) & (c == pl.num_programs(1) - 1))
    def _():
        ones = jnp.full((SUB, total.shape[1]), -0.5, F32)
        here = lax.dot_general(
            ones, total[...], dims, precision=lax.Precision.HIGHEST, preferred_element_type=F32
        )
        mine = lax.broadcasted_iota(jnp.int32, (SUB, members), 0) == cycle
        out_ref[...] = jnp.where(mine, here, first_ref[...])


CHEAP = pl.CostEstimate(flops=1000, transcendentals=0, bytes_accessed=1000)


def shape(*dims):
    return jax.ShapeDtypeStruct(dims, F32)


def call(kernel, outs, scratch=(), scalars=0, resident=10, limit=16, far=(), name=None):
    def run(*args):
        args = args[:scalars] + tuple(
            pltpu.with_memory_space_constraint(x, pltpu.VMEM) if i < resident else x
            for i, x in enumerate(args[scalars:])
        )
        specs = [pl.BlockSpec(memory_space=pltpu.SMEM)] * scalars
        specs += [pl.BlockSpec(memory_space=pltpu.VMEM)] * (len(args) - scalars)
        return pl.pallas_call(
            kernel,
            out_shape=[pltpu.HBM(o.shape, F32) if i in far else o for i, o in enumerate(outs)],
            in_specs=specs,
            out_specs=[pl.BlockSpec(memory_space=pltpu.VMEM)] * len(outs),
            scratch_shapes=list(scratch),
            compiler_params=pltpu.CompilerParams(vmem_limit_bytes=limit * 1024 * 1024),
            cost_estimate=CHEAP,
            name=name,
        )(*args)

    return run


def shards(
    vorticity, streamfunction, model_noise, offspring, footprint, observed, precision, block_rows
):
    groups, tiles = lax.axis_size("dom"), lax.axis_size("tile")
    members = offspring.shape[1]
    width = vorticity.shape[3]
    blocks = width // BW
    per = blocks // groups
    bands, observations, cells = footprint.shape[0], footprint.shape[2], footprint.shape[3]

    running = jnp.cumsum(offspring, axis=1)
    slots = jnp.arange(members, dtype=jnp.int32)
    parent = jnp.sum((running[:, None, :] <= slots[None, :, None]).astype(jnp.int32), axis=2)
    parent = jnp.minimum(parent, members - 1)
    edge = jnp.stack([lax.axis_index("tile"), jnp.int32(tiles)]).astype(jnp.int32)

    up = [(i, i + 1) for i in range(tiles - 1)]
    down = [(i + 1, i) for i in range(tiles - 1)]
    params = pltpu.CompilerParams(vmem_limit_bytes=VMEM_LIMIT)

    def pack(field, *noise):
        half = (MEM, LAYERS, SUB, width)
        return pl.pallas_call(
            functools.partial(pack_field, blocks=blocks, noisy=bool(noise)),
            grid=(2,),
            in_specs=[pl.BlockSpec(half, lambda i: (0, 0, i, 0))]
            + [pl.BlockSpec((1,) + half, lambda i: (0, 0, 0, i, 0))] * len(noise),
            out_specs=[
                pl.BlockSpec((SUB * FULL, BW), lambda i: (i, 0)),
                pl.BlockSpec((STEPS * FULL, BW), lambda i: (0, 0)),
                pl.BlockSpec((STEPS * FULL, BW), lambda i: (0, 0)),
            ],
            out_shape=[shape(ROWS * FULL, BW), shape(STEPS * FULL, BW), shape(STEPS * FULL, BW)],
            scratch_shapes=[pltpu.VMEM((SUB * FULL, BW), F32)],
            compiler_params=params,
            cost_estimate=CHEAP,
            name="pack_q" if noise else "pack_psi",
        )(field, *noise)

    p_main, p_up, p_down = pack(streamfunction)
    vorticity, p_up, p_down = lax.optimization_barrier((vorticity, p_up, p_down))
    p_below = lax.ppermute(p_up, "tile", up)
    p_above = lax.ppermute(p_down, "tile", down)
    q_main, q_up, q_down = pack(vorticity, model_noise)
    q_below = lax.ppermute(q_up, "tile", up)
    q_above = lax.ppermute(q_down, "tile", down)

    later_noise, p_below, p_above = lax.optimization_barrier((model_noise, p_below, p_above))
    noise = pl.pallas_call(
        functools.partial(pack_noise, groups=groups, per=per),
        grid=(1,),
        in_specs=[pl.BlockSpec((1, MEM, LAYERS, ROWS, width), lambda i: (1, 0, 0, 0, 0))],
        out_specs=pl.BlockSpec((groups, MEM, per * 4 + 1, SUB, BW), lambda i: (0, 0, 0, 0, 0)),
        out_shape=shape(groups, MEM, per * 4 + 1, SUB, BW),
        scratch_shapes=[pltpu.VMEM((ROWS * FULL, BW), F32)],
        compiler_params=params,
        cost_estimate=CHEAP,
        name="pack_noise",
    )(later_noise)
    noise, q_below, q_above = lax.optimization_barrier((noise, q_below, q_above))
    noise = lax.all_to_all(noise, "dom", split_axis=0, concat_axis=0, tiled=True)
    noise = noise.reshape(members, (per * 4 + 1) * SUB, BW)

    work = [
        pltpu.VMEM((DEEP * 4, PARTS * SUB, BW), F32),
        pltpu.VMEM((DEEP * 4, PARTS * SUB, BW), F32),
        pltpu.VMEM((8, PARTS * SUB, BW), F32),
        pltpu.VMEM((2 * ROWS * FULL, BW), F32),
    ]
    q_sent, p_sent = call(
        functools.partial(advance_members, groups=groups, per=per),
        [shape(groups, MEM, per * 4 + 1, SUB, BW)] * 2,
        work,
        scalars=1,
        resident=2,
        limit=32,
        far=(0, 1),
        name="advance_members",
    )(edge, q_main, p_main, q_below, p_below, q_above, p_above)
    beside = STEPS * 2 * HALF + 2 * members
    pieces = [shape(ROWS * 2 * HALF, BW), shape(8 * members, BW), shape(beside, BW), shape(beside, BW)]

    def spread(sent):
        owned = lax.all_to_all(sent, "dom", split_axis=0, concat_axis=0, tiled=True)
        return owned.reshape(members, (per * 4 + 1) * SUB, BW)

    def exchange(owned, noise=()):
        extra = [] if noise else [shape(per, ROWS * members, BW)]
        main, edges, to_up, to_down, *surface = call(
            functools.partial(resample, members=members, per=per, noisy=len(noise)),
            pieces + extra,
            [pltpu.VMEM((ROWS * FULL, BW), F32)],
            scalars=1,
            far=() if noise else (0, 1, 4),
            name="resample_q" if noise else "resample_psi",
        )(parent[0], owned, *noise)
        below = lax.ppermute(to_up, "tile", up)
        above = lax.ppermute(to_down, "tile", down)
        return main, edges, below, above, *surface

    p_sent, noise = lax.optimization_barrier((p_sent, noise))
    p_owned = spread(p_sent)
    q_sent, p_owned = lax.optimization_barrier((q_sent, p_owned))
    q_owned = spread(q_sent)
    p_main, p_edge, p_below, p_above, surface = exchange(p_owned)
    q_main, q_edge, q_below, q_above = exchange(q_owned, (noise,))

    def likelihood(cycle, surface, logs):
        small = pl.BlockSpec((1, per, observations), lambda a, c: (a, 0, 0))
        table = pl.BlockSpec((SUB, members), lambda a, c: (0, 0))
        return pl.pallas_call(
            functools.partial(score, members=members, cycle=cycle),
            grid=(bands, per),
            in_specs=[
                pl.BlockSpec(memory_space=pltpu.SMEM),
                pl.BlockSpec((per, ROWS * members, BW), lambda a, c: (0, 0, 0)),
                pl.BlockSpec((1, 1, observations, cells), lambda a, c: (a, c, 0, 0)),
                small,
                small,
                table,
            ],
            out_specs=table,
            out_shape=shape(SUB, members),
            scratch_shapes=[
                pltpu.VMEM((2 * members, cells), jnp.bfloat16),
                pltpu.VMEM((members, observations), F32),
            ],
            compiler_params=params,
            cost_estimate=CHEAP,
            name="score",
        )(block_rows, surface, footprint, observed, precision, logs)

    logs = likelihood(0, surface, jnp.zeros((SUB, members), F32))
    p_main, logs = lax.optimization_barrier((p_main, logs))

    back, surface = call(
        functools.partial(advance_columns, members=members, per=per),
        [shape(members, per * 8, SUB, BW), shape(per, ROWS * members, BW)],
        work + [pltpu.VMEM((members // SUB * 2, BW, BW), F32)],
        scalars=2,
        limit=32,
        far=(0,),
        name="advance_columns",
    )(edge, parent[1], q_main, p_main, q_edge, p_edge, q_below, p_below, q_above, p_above)
    back = back.reshape(groups, MEM, per * 64, BW)
    mine = lax.all_to_all(back, "dom", split_axis=0, concat_axis=0, tiled=True)
    loglik = likelihood(1, surface, logs)

    q_out, psi_out = call(
        functools.partial(unpack_state, groups=groups, per=per),
        [shape(MEM, LAYERS, ROWS, width)] * 2,
        limit=12,
        name="unpack_state",
    )(mine)

    for axis, size in (("tile", tiles), ("dom", groups)):
        hop = 1
        while hop < size:
            pairs = [(i, i ^ hop) for i in range(size)]
            loglik = loglik + lax.ppermute(loglik, axis, pairs)
            hop *= 2
    loglik = loglik[:CYCLES]
    total_obs = observed.size * groups * tiles
    mean_loglik = loglik / total_obs
    highest = jnp.max(loglik, axis=1, keepdims=True)
    scaled = jnp.exp(loglik - highest)
    weights = scaled / jnp.sum(scaled, axis=1, keepdims=True)
    return (q_out, psi_out, mean_loglik, weights)


def solution(mesh):
    return jax.shard_map(
        shards,
        mesh=mesh,
        in_specs=(
            P("dom", None, "tile", None),
            P("dom", None, "tile", None),
            P(None, "dom", None, "tile", None),
            P(),
            P("tile", "dom", None, None),
            P("tile", "dom", None),
            P("tile", "dom", None),
            P("tile", "dom"),
        ),
        out_specs=(P("dom", None, "tile", None), P("dom", None, "tile", None), P(), P()),
        check_vma=False,
    )
```

```python
import functools

import jax
import jax.numpy as jnp
from jax import lax
from jax.experimental import pallas as pl
from jax.experimental.pallas import tpu as pltpu
from jax.sharding import PartitionSpec as P

STEPS = 6
CYCLES = 2
BW = 128
BR = 8
ROWS = 16
MEM = 4
LAYERS = 2
SUB = 8
SEG = 16
F32 = jnp.float32
VMEM_LIMIT = 20 * 1024 * 1024
DRAG_STEP = 0.1 * 0.2
HALF = 64
PARTS = 10
QUAD = ROWS // 4
DEEP = ROWS + 2 * STEPS
FULL = 2 * HALF


def lanes():
    return lax.broadcasted_iota(jnp.int32, (SUB, BW), 1)


def lane_roll(x, shift):
    return pltpu.roll(x, shift % BW, axis=1)


def halo_pack(take):
    segment = ((lanes() + SEG // 2) // SEG) % SUB
    lower = lanes() < BW // 2
    packed = None
    for j in range(QUAD):
        before, after = take(j)
        edge = lane_roll(jnp.where(lower, after, before), SEG * j)
        packed = edge if packed is None else jnp.where(segment == j, edge, packed)
    return packed


def wide_roll(x, shift):
    return pltpu.roll(x, shift % BW, axis=1)


def lower_half(rows):
    return lax.broadcasted_iota(jnp.int32, (rows, BW), 1) < HALF


def by_layer(turned):
    top, bottom = turned[:HALF], turned[HALF:]
    low = lower_half(HALF)
    return (
        jnp.where(low, top, wide_roll(bottom, HALF)),
        jnp.where(low, wide_roll(top, HALF), bottom),
    )


def to_layers(first, second):
    low = lower_half(HALF)
    top = jnp.where(low, first, wide_roll(second, HALF))
    bottom = jnp.where(low, wide_roll(first, HALF), second)
    return jnp.concatenate([top, bottom], axis=0)


def pack_field(*refs, blocks, noisy):
    x_ref, (main_ref, up_ref, down_ref, work) = refs[0], refs[-4:]
    g = pl.program_id(0)
    for b in range(blocks):
        cols = slice(b * BW, (b + 1) * BW)
        for m in range(MEM):
            for l in range(LAYERS):
                value = x_ref[m, l, :, cols]
                if noisy:
                    value = value + refs[1][0, m, l, :, cols]
                work[pl.ds(l * HALF + b * MEM + m, SUB, stride=FULL), :] = value
    for r in range(SUB):
        for l, part in enumerate(by_layer(work[r * FULL : (r + 1) * FULL, :].T)):
            main_ref[(r * 2 + l) * HALF : (r * 2 + l + 1) * HALF, :] = part

    @pl.when(g == 0)
    def _():
        down_ref[...] = main_ref[: STEPS * FULL, :]

    @pl.when(g == 1)
    def _():
        up_ref[...] = main_ref[(SUB - STEPS) * FULL :, :]


def send_rows(work, base, out_ref, groups, per):
    blocks = groups * per
    for m in range(MEM):
        for d in range(groups):
            def rows(block, v):
                s = base + v * 4 * FULL + block % blocks * MEM + m
                return work[pl.ds(s, SUB, stride=HALF), :]

            for c in range(per):
                for v in range(QUAD):
                    out_ref[d, m, c * QUAD + v] = rows(d * per + c, v)
            out_ref[d, m, per * QUAD] = halo_pack(
                lambda v: (rows(d * per - 1, v), rows(d * per + per, v))
            )


def pack_noise(n_ref, out_ref, work, *, groups, per):
    for b in range(groups * per):
        for m in range(MEM):
            for l in range(LAYERS):
                for g in range(ROWS // SUB):
                    s = g * SUB * FULL + l * HALF + b * MEM + m
                    work[pl.ds(s, SUB, stride=FULL), :] = n_ref[
                        0, m, l, g * SUB : (g + 1) * SUB, b * BW : (b + 1) * BW
                    ]
    send_rows(work, 0, out_ref, groups, per)


def place(natural, slot, dst, plane, body, left, right):
    natural[slot, :SUB, :] = left
    natural[slot, SUB : SUB + HALF, :] = body
    natural[slot, SUB + HALF :, :] = right
    for j in range(PARTS):
        dst[plane, j * SUB : (j + 1) * SUB, :] = natural[slot, pl.ds(j, SUB, stride=PARTS), :]


def margins(body, unit, left_end, right_end):
    lane = lanes()
    first, last = body[:SUB], body[HALF - SUB :]
    left = jnp.where(lane < HALF, wide_roll(last, HALF + unit), wide_roll(last, HALF))
    right = jnp.where(lane < HALF, wide_roll(first, HALF), wide_roll(first, HALF - unit))
    return jnp.where(lane < unit, left_end, left), jnp.where(lane >= BW - unit, right_end, right)


def run_steps(edge, first, second):
    zero = jnp.zeros((STEPS * 4, PARTS * SUB, BW), F32)

    @pl.when(edge[0] == 0)
    def _():
        second[: STEPS * 4] = zero

    @pl.when(edge[0] == edge[1] - 1)
    def _():
        second[(STEPS + ROWS) * 4 :] = zero

    src, dst = first, second
    for step in range(STEPS):
        low = jnp.where(edge[0] == 0, STEPS, step + 1)
        high = jnp.where(edge[0] == edge[1] - 1, STEPS + ROWS, DEEP - 1 - step)

        def body(i, _, src=src, dst=dst):
            for l in range(LAYERS):
                def load(f, j, di=0, layer=l):
                    return src[((i + di) * 2 + layer) * 2 + f, j * SUB : (j + 1) * SUB, :]

                west = tuple(pltpu.roll(load(f, PARTS - 1), 1, axis=0) for f in range(2))
                final = tuple(pltpu.roll(load(f, 0), SUB - 1, axis=0) for f in range(2))
                here = (load(0, 0), load(1, 0))
                for j in range(PARTS):
                    east = (load(0, j + 1), load(1, j + 1)) if j + 1 < PARTS else final
                    q, psi = here
                    psi_n, psi_s = load(1, j, 1), load(1, j, -1)
                    around = (psi_n + psi_s) + (east[1] + west[1])
                    along = east[1] - west[1]
                    psi_new = (around + load(1, j, 0, 1 - l) - q) * 0.2
                    change = along * ((load(0, j, 1) - load(0, j, -1)) + 1.0) - (
                        psi_n - psi_s
                    ) * (east[0] - west[0])
                    q_new = q - 0.025 * change
                    if l == 1:
                        q_new = q_new - DRAG_STEP * (around - 4.0 * psi)
                    dst[(i * 2 + l) * 2, j * SUB : (j + 1) * SUB, :] = q_new
                    dst[(i * 2 + l) * 2 + 1, j * SUB : (j + 1) * SUB, :] = psi_new
                    west, here = here, east
            return 0

        lax.fori_loop(low, high, body, 0)
        src, dst = dst, src
    return src


def turn_back(src, natural, turned):
    def body(pair, _):
        for turn in range(4):
            r, f = 2 * pair + turn // 2, turn % 2
            parts = []
            for l in range(LAYERS):
                slot = turn * 2 + l
                plane = ((r + STEPS) * 2 + l) * 2 + f
                for j in range(PARTS):
                    natural[slot, pl.ds(j, SUB, stride=PARTS), :] = src[
                        plane, j * SUB : (j + 1) * SUB, :
                    ]
                parts.append(natural[slot, SUB : SUB + HALF, :])
            s = pl.multiple_of((f * ROWS + r) * FULL, FULL)
            turned[pl.ds(s, FULL), :] = to_layers(*parts).T
        return 0

    lax.fori_loop(0, ROWS // 2, body, 0)


def advance_members(
    edge, q_main, p_main, q_up, p_up, q_down, p_down, q_out, p_out,
    first, second, natural, turned, *, groups, per
):
    def fill(refs, count, start):
        def body(pair, _):
            for turn in range(4):
                r, f = 2 * pair + turn // 2, turn % 2
                for l in range(LAYERS):
                    s = pl.multiple_of((r * 2 + l) * HALF, HALF)
                    value = refs[f][pl.ds(s, HALF), :]
                    ends = wide_roll(value[HALF - SUB :], MEM), wide_roll(value[:SUB], -MEM)
                    plane = ((r + start) * 2 + l) * 2 + f
                    place(natural, turn * 2 + l, first, plane, value, *margins(value, MEM, *ends))
            return 0

        lax.fori_loop(0, count // 2, body, 0)

    fill((q_main, p_main), ROWS, STEPS)
    fill((q_up, p_up), STEPS, 0)
    fill((q_down, p_down), STEPS, STEPS + ROWS)
    src = run_steps(edge, first, second)
    turn_back(src, natural, turned)
    send_rows(turned, 0, q_out, groups, per)
    send_rows(turned, ROWS * FULL, p_out, groups, per)


def resample(parent, x_ref, *refs, members, per, noisy):
    main_ref, edge_ref, up_ref, down_ref = refs[noisy : noisy + 4]
    work = refs[-1]

    def one(k, _):
        p = parent[k]
        beside = x_ref[p, per * 32 :, :]
        for c in range(per):
            for v in range(QUAD):
                value = x_ref[p, (c * QUAD + v) * SUB : (c * QUAD + v + 1) * SUB, :]
                if noisy:
                    value = value + refs[0][k, (c * QUAD + v) * SUB : (c * QUAD + v + 1) * SUB, :]
                work[pl.ds(v * 4 * FULL + c * members + k, SUB, stride=HALF), :] = value
            if not noisy:
                for g in range(2):
                    refs[-2][c, pl.ds(g * SUB * members + k, SUB, stride=members), :] = x_ref[
                        k, pl.ds(c * 32 + g * 16, SUB, stride=2), :
                    ]
        if noisy:
            beside = beside + refs[0][k, per * 32 :, :]
        edge_ref[pl.ds(k, SUB, stride=members), :] = beside
        return 0

    lax.fori_loop(0, members, one, 0)
    for r in range(ROWS):
        for l, part in enumerate(by_layer(work[r * FULL : (r + 1) * FULL, :].T)):
            s = (r * 2 + l) * HALF
            main_ref[s : s + HALF, :] = part
            if r < STEPS:
                down_ref[s : s + HALF, :] = part
            if r >= ROWS - STEPS:
                s -= (ROWS - STEPS) * 2 * HALF
                up_ref[s : s + HALF, :] = part
    count = 2 * members
    segment = ((lax.broadcasted_iota(jnp.int32, (count, BW), 1) + SEG // 2) // SEG) % SUB
    for ref, start in ((up_ref, ROWS - STEPS), (down_ref, 0)):
        sides = None
        for i in range(STEPS):
            v, q = divmod(start + i, 4)
            rows = wide_roll(edge_ref[q * count : (q + 1) * count, :], SEG * (i - v))
            sides = rows if sides is None else jnp.where(segment == i, rows, sides)
        ref[STEPS * 2 * HALF :, :] = sides


def advance_columns(
    edge, parent, q_main, p_main, q_edge, p_edge, q_up, p_up, q_down, p_down, out_ref, z_ref,
    first, second, natural, turned, sides, *, members, per
):
    top = STEPS * 2 * HALF
    own = 8 * members // BW
    beside = own // 2
    for f, ref in enumerate((q_edge, p_edge)):
        for i in range(own):
            sides[f * own + i] = ref[i * BW : (i + 1) * BW, :].T
    for n, refs in enumerate(((q_up, p_up), (q_down, p_down))):
        both = jnp.concatenate([refs[0][top:, :], refs[1][top:, :]], axis=0)
        for i in range(beside):
            sides[2 * own + n * beside + i] = both[i * BW : (i + 1) * BW, :].T

    def put(source, r, row, f, l, base, index, group, turn):
        value = source[pl.ds(pl.multiple_of((r * 2 + l) * HALF, HALF), HALF), :]
        matrix, offset = base + index * members // BW, index * members % BW
        before = pl.multiple_of((group * SEG + BW - SUB) % BW, SUB)
        after = pl.multiple_of(group * SEG, SUB)
        ends = (
            wide_roll(sides[matrix, pl.ds(before, SUB), :], -offset),
            wide_roll(sides[matrix, pl.ds(after, SUB), :], BW - members - offset),
        )
        plane = (row * 2 + l) * 2 + f
        place(natural, turn * 4 + f * 2 + l, first, plane, value, *margins(value, members, *ends))

    def rows_own(v, _):
        for q in range(4):
            for f, source in enumerate((q_main, p_main)):
                for l in range(LAYERS):
                    put(source, 4 * v + q, 4 * v + q + STEPS, f, l, f * own, q * 2 + l, v, q % 2)
        return 0

    lax.fori_loop(0, QUAD, rows_own, 0)

    def rows_beside(i, _):
        for n, refs in enumerate(((q_up, p_up), (q_down, p_down))):
            for f in range(2):
                for l in range(LAYERS):
                    row = i + n * (STEPS + ROWS)
                    put(refs[f], i, row, f, l, 2 * own + n * beside, f * 2 + l, i, n)
        return 0

    lax.fori_loop(0, STEPS, rows_beside, 0)
    src = run_steps(edge, first, second)
    turn_back(src, natural, turned)

    def one(k, _):
        p = parent[k]
        for c in range(per):
            for f in range(2):
                for v in range(QUAD):
                    s = f * ROWS * FULL + v * 4 * FULL + c * members + p
                    out_ref[k, (c * 2 + f) * QUAD + v] = turned[pl.ds(s, SUB, stride=HALF), :]
        return 0

    lax.fori_loop(0, members, one, 0)
    for c in range(per):
        for r in range(ROWS):
            s = (ROWS + r) * FULL + c * members
            z_ref[c, r * members : (r + 1) * members, :] = turned[s : s + members, :]


def unpack_state(y_ref, q_ref, p_ref, *, groups, per):
    for d in range(groups):
        for c in range(per):
            b = d * per + c
            for m, l in [(m, l) for m in range(MEM) for l in range(LAYERS)]:
                for g in range(ROWS // SUB):
                    rows, cols = slice(g * SUB, (g + 1) * SUB), slice(b * BW, (b + 1) * BW)
                    s = c * 64 + g * 16 + l
                    q_ref[m, l, rows, cols] = y_ref[d, m, pl.ds(s, SUB, stride=2), :]
                    p_ref[m, l, rows, cols] = y_ref[d, m, pl.ds(s + 32, SUB, stride=2), :]


def score(rows_ref, z_ref, f_ref, o_ref, w_ref, first_ref, out_ref, patch, total, *, members, cycle):
    a, c = pl.program_id(0), pl.program_id(1)

    @pl.when((a == 0) & (c == 0))
    def _():
        total[...] = jnp.zeros_like(total)

    start = rows_ref[a, c]
    for r in range(BR):
        s = pl.multiple_of((start + r) * members, SUB)
        part = z_ref[c, pl.ds(s, members), :]
        high = part.astype(jnp.bfloat16)
        patch[:members, r * BW : (r + 1) * BW] = high
        patch[members:, r * BW : (r + 1) * BW] = (part - high.astype(F32)).astype(jnp.bfloat16)

    weights = f_ref[0, 0]
    high = weights.astype(jnp.bfloat16)
    low = (weights - high.astype(F32)).astype(jnp.bfloat16)
    dims = (((1,), (1,)), ((), ()))
    main = lax.dot_general(patch[...], high, dims, preferred_element_type=F32)
    rest = lax.dot_general(patch[:members, :], low, dims, preferred_element_type=F32)
    predicted = main[:members] + (main[members:] + rest)
    miss = o_ref[0, pl.ds(c, 1), :] - predicted
    total[...] += w_ref[0, pl.ds(c, 1), :] * miss * miss

    @pl.when((a == pl.num_programs(0) - 1) & (c == pl.num_programs(1) - 1))
    def _():
        ones = jnp.full((SUB, total.shape[1]), -0.5, F32)
        here = lax.dot_general(
            ones, total[...], dims, precision=lax.Precision.HIGHEST, preferred_element_type=F32
        )
        mine = lax.broadcasted_iota(jnp.int32, (SUB, members), 0) == cycle
        out_ref[...] = jnp.where(mine, here, first_ref[...])


CHEAP = pl.CostEstimate(flops=1000, transcendentals=0, bytes_accessed=1000)


def shape(*dims):
    return jax.ShapeDtypeStruct(dims, F32)


def call(kernel, outs, scratch=(), scalars=0, resident=10, limit=16, far=(), name=None):
    def run(*args):
        args = args[:scalars] + tuple(
            pltpu.with_memory_space_constraint(x, pltpu.VMEM if i < resident else pltpu.HBM)
            for i, x in enumerate(args[scalars:])
        )
        specs = [pl.BlockSpec(memory_space=pltpu.SMEM)] * scalars
        specs += [pl.BlockSpec(memory_space=pltpu.VMEM)] * (len(args) - scalars)
        return pl.pallas_call(
            kernel,
            out_shape=[pltpu.HBM(o.shape, F32) if i in far else o for i, o in enumerate(outs)],
            in_specs=specs,
            out_specs=[pl.BlockSpec(memory_space=pltpu.VMEM)] * len(outs),
            scratch_shapes=list(scratch),
            compiler_params=pltpu.CompilerParams(vmem_limit_bytes=limit * 1024 * 1024),
            cost_estimate=CHEAP,
            name=name,
        )(*args)

    return run


def shards(
    vorticity, streamfunction, model_noise, offspring, footprint, observed, precision, block_rows
):
    groups, tiles = lax.axis_size("dom"), lax.axis_size("tile")
    members = offspring.shape[1]
    width = vorticity.shape[3]
    blocks = width // BW
    per = blocks // groups
    bands, observations, cells = footprint.shape[0], footprint.shape[2], footprint.shape[3]

    running = jnp.cumsum(offspring, axis=1)
    slots = jnp.arange(members, dtype=jnp.int32)
    parent = jnp.sum((running[:, None, :] <= slots[None, :, None]).astype(jnp.int32), axis=2)
    parent = jnp.minimum(parent, members - 1)
    edge = jnp.stack([lax.axis_index("tile"), jnp.int32(tiles)]).astype(jnp.int32)

    up = [(i, i + 1) for i in range(tiles - 1)]
    down = [(i + 1, i) for i in range(tiles - 1)]
    params = pltpu.CompilerParams(vmem_limit_bytes=VMEM_LIMIT)

    def pack(field, *noise):
        half = (MEM, LAYERS, SUB, width)
        return pl.pallas_call(
            functools.partial(pack_field, blocks=blocks, noisy=bool(noise)),
            grid=(2,),
            in_specs=[pl.BlockSpec(half, lambda i: (0, 0, i, 0))]
            + [pl.BlockSpec((1,) + half, lambda i: (0, 0, 0, i, 0))] * len(noise),
            out_specs=[
                pl.BlockSpec((SUB * FULL, BW), lambda i: (i, 0)),
                pl.BlockSpec((STEPS * FULL, BW), lambda i: (0, 0)),
                pl.BlockSpec((STEPS * FULL, BW), lambda i: (0, 0)),
            ],
            out_shape=[shape(ROWS * FULL, BW), shape(STEPS * FULL, BW), shape(STEPS * FULL, BW)],
            scratch_shapes=[pltpu.VMEM((SUB * FULL, BW), F32)],
            compiler_params=params,
            cost_estimate=CHEAP,
            name="pack_q" if noise else "pack_psi",
        )(field, *noise)

    p_main, p_up, p_down = pack(streamfunction)
    vorticity, p_up, p_down = lax.optimization_barrier((vorticity, p_up, p_down))
    p_below = lax.ppermute(p_up, "tile", up)
    p_above = lax.ppermute(p_down, "tile", down)
    q_main, q_up, q_down = pack(vorticity, model_noise)
    q_below = lax.ppermute(q_up, "tile", up)
    q_above = lax.ppermute(q_down, "tile", down)

    later_noise, p_below, p_above = lax.optimization_barrier((model_noise, p_below, p_above))
    noise = pl.pallas_call(
        functools.partial(pack_noise, groups=groups, per=per),
        grid=(1,),
        in_specs=[pl.BlockSpec((1, MEM, LAYERS, ROWS, width), lambda i: (1, 0, 0, 0, 0))],
        out_specs=pl.BlockSpec((groups, MEM, per * 4 + 1, SUB, BW), lambda i: (0, 0, 0, 0, 0)),
        out_shape=shape(groups, MEM, per * 4 + 1, SUB, BW),
        scratch_shapes=[pltpu.VMEM((ROWS * FULL, BW), F32)],
        compiler_params=params,
        cost_estimate=CHEAP,
        name="pack_noise",
    )(later_noise)
    noise, q_below, q_above = lax.optimization_barrier((noise, q_below, q_above))
    noise = lax.all_to_all(noise, "dom", split_axis=0, concat_axis=0, tiled=True)
    noise = noise.reshape(members, (per * 4 + 1) * SUB, BW)

    work = [
        pltpu.VMEM((DEEP * 4, PARTS * SUB, BW), F32),
        pltpu.VMEM((DEEP * 4, PARTS * SUB, BW), F32),
        pltpu.VMEM((8, PARTS * SUB, BW), F32),
        pltpu.VMEM((2 * ROWS * FULL, BW), F32),
    ]
    q_sent, p_sent = call(
        functools.partial(advance_members, groups=groups, per=per),
        [shape(groups, MEM, per * 4 + 1, SUB, BW)] * 2,
        work,
        scalars=1,
        resident=2,
        limit=32,
        far=(0, 1),
        name="advance_members",
    )(edge, q_main, p_main, q_below, p_below, q_above, p_above)
    beside = STEPS * 2 * HALF + 2 * members
    pieces = [shape(ROWS * 2 * HALF, BW), shape(8 * members, BW), shape(beside, BW), shape(beside, BW)]

    def spread(sent):
        owned = lax.all_to_all(sent, "dom", split_axis=0, concat_axis=0, tiled=True)
        return owned.reshape(members, (per * 4 + 1) * SUB, BW)

    def exchange(owned, noise=()):
        extra = [] if noise else [shape(per, ROWS * members, BW)]
        main, edges, to_up, to_down, *surface = call(
            functools.partial(resample, members=members, per=per, noisy=len(noise)),
            pieces + extra,
            [pltpu.VMEM((ROWS * FULL, BW), F32)],
            scalars=1,
            far=() if noise else (0, 1, 4),
            name="resample_q" if noise else "resample_psi",
        )(parent[0], owned, *noise)
        below = lax.ppermute(to_up, "tile", up)
        above = lax.ppermute(to_down, "tile", down)
        return main, edges, below, above, *surface

    p_sent, noise = lax.optimization_barrier((p_sent, noise))
    p_owned = spread(p_sent)
    q_sent, p_owned = lax.optimization_barrier((q_sent, p_owned))
    q_owned = spread(q_sent)
    p_main, p_edge, p_below, p_above, surface = exchange(p_owned)
    q_main, q_edge, q_below, q_above = exchange(q_owned, (noise,))

    stored = pltpu.with_memory_space_constraint(footprint, pltpu.HBM)

    def likelihood(cycle, surface, logs):
        small = pl.BlockSpec((1, per, observations), lambda a, c: (a, 0, 0))
        table = pl.BlockSpec((SUB, members), lambda a, c: (0, 0))
        return pl.pallas_call(
            functools.partial(score, members=members, cycle=cycle),
            grid=(bands, per),
            in_specs=[
                pl.BlockSpec(memory_space=pltpu.SMEM),
                pl.BlockSpec((per, ROWS * members, BW), lambda a, c: (0, 0, 0)),
                pl.BlockSpec((1, 1, observations, cells), lambda a, c: (a, c, 0, 0)),
                small,
                small,
                table,
            ],
            out_specs=table,
            out_shape=shape(SUB, members),
            scratch_shapes=[
                pltpu.VMEM((2 * members, cells), jnp.bfloat16),
                pltpu.VMEM((members, observations), F32),
            ],
            compiler_params=params,
            cost_estimate=CHEAP,
            name="score",
        )(block_rows, surface, stored, observed, precision, logs)

    logs = likelihood(0, surface, jnp.zeros((SUB, members), F32))
    p_main, logs = lax.optimization_barrier((p_main, logs))

    back, surface = call(
        functools.partial(advance_columns, members=members, per=per),
        [shape(members, per * 8, SUB, BW), shape(per, ROWS * members, BW)],
        work + [pltpu.VMEM((members // SUB * 2, BW, BW), F32)],
        scalars=2,
        limit=32,
        far=(0,),
        name="advance_columns",
    )(edge, parent[1], q_main, p_main, q_edge, p_edge, q_below, p_below, q_above, p_above)
    back = back.reshape(groups, MEM, per * 64, BW)
    mine = lax.all_to_all(back, "dom", split_axis=0, concat_axis=0, tiled=True)
    loglik = likelihood(1, surface, logs)

    q_out, psi_out = call(
        functools.partial(unpack_state, groups=groups, per=per),
        [shape(MEM, LAYERS, ROWS, width)] * 2,
        limit=12,
        name="unpack_state",
    )(mine)

    for axis, size in (("tile", tiles), ("dom", groups)):
        hop = 1
        while hop < size:
            pairs = [(i, i ^ hop) for i in range(size)]
            loglik = loglik + lax.ppermute(loglik, axis, pairs)
            hop *= 2
    loglik = loglik[:CYCLES]
    total_obs = observed.size * groups * tiles
    mean_loglik = loglik / total_obs
    highest = jnp.max(loglik, axis=1, keepdims=True)
    scaled = jnp.exp(loglik - highest)
    weights = scaled / jnp.sum(scaled, axis=1, keepdims=True)
    return (q_out, psi_out, mean_loglik, weights)


def solution(mesh):
    return jax.shard_map(
        shards,
        mesh=mesh,
        in_specs=(
            P("dom", None, "tile", None),
            P("dom", None, "tile", None),
            P(None, "dom", None, "tile", None),
            P(),
            P("tile", "dom", None, None),
            P("tile", "dom", None),
            P("tile", "dom", None),
            P("tile", "dom"),
        ),
        out_specs=(P("dom", None, "tile", None), P("dom", None, "tile", None), P(), P()),
        check_vma=False,
    )
```

```python
import functools

import jax
import jax.numpy as jnp
from jax import lax
from jax.experimental import pallas as pl
from jax.experimental.pallas import tpu as pltpu
from jax.sharding import PartitionSpec as P

STEPS = 6
CYCLES = 2
BW = 128
BR = 8
ROWS = 16
MEM = 4
LAYERS = 2
SUB = 8
SEG = 16
F32 = jnp.float32
VMEM_LIMIT = 20 * 1024 * 1024
DRAG_STEP = 0.1 * 0.2
HALF = 64
PARTS = 10
QUAD = ROWS // 4
DEEP = ROWS + 2 * STEPS
FULL = 2 * HALF


def lanes():
    return lax.broadcasted_iota(jnp.int32, (SUB, BW), 1)


def lane_roll(x, shift):
    return pltpu.roll(x, shift % BW, axis=1)


def halo_pack(take):
    segment = ((lanes() + SEG // 2) // SEG) % SUB
    lower = lanes() < BW // 2
    packed = None
    for j in range(QUAD):
        before, after = take(j)
        edge = lane_roll(jnp.where(lower, after, before), SEG * j)
        packed = edge if packed is None else jnp.where(segment == j, edge, packed)
    return packed


def wide_roll(x, shift):
    return pltpu.roll(x, shift % BW, axis=1)


def lower_half(rows):
    return lax.broadcasted_iota(jnp.int32, (rows, BW), 1) < HALF


def by_layer(turned):
    top, bottom = turned[:HALF], turned[HALF:]
    low = lower_half(HALF)
    return (
        jnp.where(low, top, wide_roll(bottom, HALF)),
        jnp.where(low, wide_roll(top, HALF), bottom),
    )


def to_layers(first, second):
    low = lower_half(HALF)
    top = jnp.where(low, first, wide_roll(second, HALF))
    bottom = jnp.where(low, wide_roll(first, HALF), second)
    return jnp.concatenate([top, bottom], axis=0)


def pack_field(*refs, blocks, noisy):
    x_ref, (main_ref, up_ref, down_ref, work) = refs[0], refs[-4:]
    g = pl.program_id(0)
    for b in range(blocks):
        cols = slice(b * BW, (b + 1) * BW)
        for m in range(MEM):
            for l in range(LAYERS):
                value = x_ref[m, l, :, cols]
                if noisy:
                    value = value + refs[1][0, m, l, :, cols]
                work[pl.ds(l * HALF + b * MEM + m, SUB, stride=FULL), :] = value
    for r in range(SUB):
        for l, part in enumerate(by_layer(work[r * FULL : (r + 1) * FULL, :].T)):
            main_ref[(r * 2 + l) * HALF : (r * 2 + l + 1) * HALF, :] = part

    @pl.when(g == 0)
    def _():
        down_ref[...] = main_ref[: STEPS * FULL, :]

    @pl.when(g == 1)
    def _():
        up_ref[...] = main_ref[(SUB - STEPS) * FULL :, :]


def send_rows(work, base, out_ref, groups, per):
    blocks = groups * per
    for m in range(MEM):
        for d in range(groups):
            def rows(block, v):
                s = base + v * 4 * FULL + block % blocks * MEM + m
                return work[pl.ds(s, SUB, stride=HALF), :]

            for c in range(per):
                for v in range(QUAD):
                    out_ref[d, m, c * QUAD + v] = rows(d * per + c, v)
            out_ref[d, m, per * QUAD] = halo_pack(
                lambda v: (rows(d * per - 1, v), rows(d * per + per, v))
            )


def pack_noise(n_ref, out_ref, work, *, groups, per):
    for b in range(groups * per):
        for m in range(MEM):
            for l in range(LAYERS):
                for g in range(ROWS // SUB):
                    s = g * SUB * FULL + l * HALF + b * MEM + m
                    work[pl.ds(s, SUB, stride=FULL), :] = n_ref[
                        0, m, l, g * SUB : (g + 1) * SUB, b * BW : (b + 1) * BW
                    ]
    send_rows(work, 0, out_ref, groups, per)


def place(natural, slot, dst, plane, body, left, right):
    natural[slot, :SUB, :] = left
    natural[slot, SUB : SUB + HALF, :] = body
    natural[slot, SUB + HALF :, :] = right
    for j in range(PARTS):
        dst[plane, j * SUB : (j + 1) * SUB, :] = natural[slot, pl.ds(j, SUB, stride=PARTS), :]


def margins(body, unit, left_end, right_end):
    lane = lanes()
    first, last = body[:SUB], body[HALF - SUB :]
    left = jnp.where(lane < HALF, wide_roll(last, HALF + unit), wide_roll(last, HALF))
    right = jnp.where(lane < HALF, wide_roll(first, HALF), wide_roll(first, HALF - unit))
    return jnp.where(lane < unit, left_end, left), jnp.where(lane >= BW - unit, right_end, right)


def run_steps(edge, first, second):
    zero = jnp.zeros((STEPS * 4, PARTS * SUB, BW), F32)

    @pl.when(edge[0] == 0)
    def _():
        second[: STEPS * 4] = zero

    @pl.when(edge[0] == edge[1] - 1)
    def _():
        second[(STEPS + ROWS) * 4 :] = zero

    src, dst = first, second
    for step in range(STEPS):
        low = jnp.where(edge[0] == 0, STEPS, step + 1)
        high = jnp.where(edge[0] == edge[1] - 1, STEPS + ROWS, DEEP - 1 - step)

        def body(i, _, src=src, dst=dst):
            for l in range(LAYERS):
                def load(f, j, di=0, layer=l):
                    return src[((i + di) * 2 + layer) * 2 + f, j * SUB : (j + 1) * SUB, :]

                west = tuple(pltpu.roll(load(f, PARTS - 1), 1, axis=0) for f in range(2))
                final = tuple(pltpu.roll(load(f, 0), SUB - 1, axis=0) for f in range(2))
                here = (load(0, 0), load(1, 0))
                for j in range(PARTS):
                    east = (load(0, j + 1), load(1, j + 1)) if j + 1 < PARTS else final
                    q, psi = here
                    psi_n, psi_s = load(1, j, 1), load(1, j, -1)
                    around = (psi_n + psi_s) + (east[1] + west[1])
                    along = east[1] - west[1]
                    psi_new = (around + load(1, j, 0, 1 - l) - q) * 0.2
                    change = along * ((load(0, j, 1) - load(0, j, -1)) + 1.0) - (
                        psi_n - psi_s
                    ) * (east[0] - west[0])
                    q_new = q - 0.025 * change
                    if l == 1:
                        q_new = q_new - DRAG_STEP * (around - 4.0 * psi)
                    dst[(i * 2 + l) * 2, j * SUB : (j + 1) * SUB, :] = q_new
                    dst[(i * 2 + l) * 2 + 1, j * SUB : (j + 1) * SUB, :] = psi_new
                    west, here = here, east
            return 0

        lax.fori_loop(low, high, body, 0)
        src, dst = dst, src
    return src


def turn_back(src, natural, turned):
    def body(pair, _):
        for turn in range(4):
            r, f = 2 * pair + turn // 2, turn % 2
            parts = []
            for l in range(LAYERS):
                slot = turn * 2 + l
                plane = ((r + STEPS) * 2 + l) * 2 + f
                for j in range(PARTS):
                    natural[slot, pl.ds(j, SUB, stride=PARTS), :] = src[
                        plane, j * SUB : (j + 1) * SUB, :
                    ]
                parts.append(natural[slot, SUB : SUB + HALF, :])
            s = pl.multiple_of((f * ROWS + r) * FULL, FULL)
            turned[pl.ds(s, FULL), :] = to_layers(*parts).T
        return 0

    lax.fori_loop(0, ROWS // 2, body, 0)


def advance_members(
    edge, q_main, p_main, q_up, p_up, q_down, p_down, q_out, p_out,
    first, second, natural, turned, *, groups, per
):
    def fill(refs, count, start):
        def body(pair, _):
            for turn in range(4):
                r, f = 2 * pair + turn // 2, turn % 2
                for l in range(LAYERS):
                    s = pl.multiple_of((r * 2 + l) * HALF, HALF)
                    value = refs[f][pl.ds(s, HALF), :]
                    ends = wide_roll(value[HALF - SUB :], MEM), wide_roll(value[:SUB], -MEM)
                    plane = ((r + start) * 2 + l) * 2 + f
                    place(natural, turn * 2 + l, first, plane, value, *margins(value, MEM, *ends))
            return 0

        lax.fori_loop(0, count // 2, body, 0)

    fill((q_main, p_main), ROWS, STEPS)
    fill((q_up, p_up), STEPS, 0)
    fill((q_down, p_down), STEPS, STEPS + ROWS)
    src = run_steps(edge, first, second)
    turn_back(src, natural, turned)
    send_rows(turned, 0, q_out, groups, per)
    send_rows(turned, ROWS * FULL, p_out, groups, per)


def resample(parent, x_ref, *refs, members, per, noisy):
    main_ref, edge_ref, up_ref, down_ref = refs[noisy : noisy + 4]
    work = refs[-1]

    def one(k, _):
        p = parent[k]
        beside = x_ref[p, per * 32 :, :]
        for c in range(per):
            for v in range(QUAD):
                value = x_ref[p, (c * QUAD + v) * SUB : (c * QUAD + v + 1) * SUB, :]
                if noisy:
                    value = value + refs[0][k, (c * QUAD + v) * SUB : (c * QUAD + v + 1) * SUB, :]
                work[pl.ds(v * 4 * FULL + c * members + k, SUB, stride=HALF), :] = value
            if not noisy:
                for g in range(2):
                    refs[-2][c, pl.ds(g * SUB * members + k, SUB, stride=members), :] = x_ref[
                        k, pl.ds(c * 32 + g * 16, SUB, stride=2), :
                    ]
        if noisy:
            beside = beside + refs[0][k, per * 32 :, :]
        edge_ref[pl.ds(k, SUB, stride=members), :] = beside
        return 0

    lax.fori_loop(0, members, one, 0)
    for r in range(ROWS):
        for l, part in enumerate(by_layer(work[r * FULL : (r + 1) * FULL, :].T)):
            s = (r * 2 + l) * HALF
            main_ref[s : s + HALF, :] = part
            if r < STEPS:
                down_ref[s : s + HALF, :] = part
            if r >= ROWS - STEPS:
                s -= (ROWS - STEPS) * 2 * HALF
                up_ref[s : s + HALF, :] = part
    count = 2 * members
    segment = ((lax.broadcasted_iota(jnp.int32, (count, BW), 1) + SEG // 2) // SEG) % SUB
    for ref, start in ((up_ref, ROWS - STEPS), (down_ref, 0)):
        sides = None
        for i in range(STEPS):
            v, q = divmod(start + i, 4)
            rows = wide_roll(edge_ref[q * count : (q + 1) * count, :], SEG * (i - v))
            sides = rows if sides is None else jnp.where(segment == i, rows, sides)
        ref[STEPS * 2 * HALF :, :] = sides


def advance_columns(
    edge, parent, q_main, p_main, q_edge, p_edge, q_up, p_up, q_down, p_down, out_ref, z_ref,
    first, second, natural, turned, sides, *, members, per
):
    top = STEPS * 2 * HALF
    own = 8 * members // BW
    beside = own // 2
    for f, ref in enumerate((q_edge, p_edge)):
        for i in range(own):
            sides[f * own + i] = ref[i * BW : (i + 1) * BW, :].T
    for n, refs in enumerate(((q_up, p_up), (q_down, p_down))):
        both = jnp.concatenate([refs[0][top:, :], refs[1][top:, :]], axis=0)
        for i in range(beside):
            sides[2 * own + n * beside + i] = both[i * BW : (i + 1) * BW, :].T

    def put(source, r, row, f, l, base, index, group, turn):
        value = source[pl.ds(pl.multiple_of((r * 2 + l) * HALF, HALF), HALF), :]
        matrix, offset = base + index * members // BW, index * members % BW
        before = pl.multiple_of((group * SEG + BW - SUB) % BW, SUB)
        after = pl.multiple_of(group * SEG, SUB)
        ends = (
            wide_roll(sides[matrix, pl.ds(before, SUB), :], -offset),
            wide_roll(sides[matrix, pl.ds(after, SUB), :], BW - members - offset),
        )
        plane = (row * 2 + l) * 2 + f
        place(natural, turn * 4 + f * 2 + l, first, plane, value, *margins(value, members, *ends))

    def rows_own(v, _):
        for q in range(4):
            for f, source in enumerate((q_main, p_main)):
                for l in range(LAYERS):
                    put(source, 4 * v + q, 4 * v + q + STEPS, f, l, f * own, q * 2 + l, v, q % 2)
        return 0

    lax.fori_loop(0, QUAD, rows_own, 0)

    def rows_beside(i, _):
        for n, refs in enumerate(((q_up, p_up), (q_down, p_down))):
            for f in range(2):
                for l in range(LAYERS):
                    row = i + n * (STEPS + ROWS)
                    put(refs[f], i, row, f, l, 2 * own + n * beside, f * 2 + l, i, n)
        return 0

    lax.fori_loop(0, STEPS, rows_beside, 0)
    src = run_steps(edge, first, second)
    turn_back(src, natural, turned)

    def one(k, _):
        p = parent[k]
        for c in range(per):
            for f in range(2):
                for v in range(QUAD):
                    s = f * ROWS * FULL + v * 4 * FULL + c * members + p
                    out_ref[k, (c * 2 + f) * QUAD + v] = turned[pl.ds(s, SUB, stride=HALF), :]
        return 0

    lax.fori_loop(0, members, one, 0)
    for c in range(per):
        for r in range(ROWS):
            s = (ROWS + r) * FULL + c * members
            z_ref[c, r * members : (r + 1) * members, :] = turned[s : s + members, :]


def unpack_state(y_ref, q_ref, p_ref, *, groups, per):
    for d in range(groups):
        for c in range(per):
            b = d * per + c
            for m, l in [(m, l) for m in range(MEM) for l in range(LAYERS)]:
                for g in range(ROWS // SUB):
                    rows, cols = slice(g * SUB, (g + 1) * SUB), slice(b * BW, (b + 1) * BW)
                    s = c * 64 + g * 16 + l
                    q_ref[m, l, rows, cols] = y_ref[d, m, pl.ds(s, SUB, stride=2), :]
                    p_ref[m, l, rows, cols] = y_ref[d, m, pl.ds(s + 32, SUB, stride=2), :]


def score(rows_ref, z_ref, f_ref, o_ref, w_ref, first_ref, out_ref, patch, total, *, members, cycle):
    a, c = pl.program_id(0), pl.program_id(1)

    @pl.when((a == 0) & (c == 0))
    def _():
        total[...] = jnp.zeros_like(total)

    start = rows_ref[a, c]
    for r in range(BR):
        s = pl.multiple_of((start + r) * members, SUB)
        part = z_ref[c, pl.ds(s, members), :]
        high = part.astype(jnp.bfloat16)
        patch[:members, r * BW : (r + 1) * BW] = high
        patch[members:, r * BW : (r + 1) * BW] = (part - high.astype(F32)).astype(jnp.bfloat16)

    weights = f_ref[0, 0]
    high = weights.astype(jnp.bfloat16)
    low = (weights - high.astype(F32)).astype(jnp.bfloat16)
    dims = (((1,), (1,)), ((), ()))
    main = lax.dot_general(patch[...], high, dims, preferred_element_type=F32)
    rest = lax.dot_general(patch[:members, :], low, dims, preferred_element_type=F32)
    predicted = main[:members] + (main[members:] + rest)
    miss = o_ref[0, pl.ds(c, 1), :] - predicted
    total[...] += w_ref[0, pl.ds(c, 1), :] * miss * miss

    @pl.when((a == pl.num_programs(0) - 1) & (c == pl.num_programs(1) - 1))
    def _():
        ones = jnp.full((SUB, total.shape[1]), -0.5, F32)
        here = lax.dot_general(
            ones, total[...], dims, precision=lax.Precision.HIGHEST, preferred_element_type=F32
        )
        mine = lax.broadcasted_iota(jnp.int32, (SUB, members), 0) == cycle
        out_ref[...] = jnp.where(mine, here, first_ref[...])


CHEAP = pl.CostEstimate(flops=1000, transcendentals=0, bytes_accessed=1000)


def shape(*dims):
    return jax.ShapeDtypeStruct(dims, F32)


def call(kernel, outs, scratch=(), scalars=0, resident=10, limit=16, far=(), name=None):
    def run(*args):
        args = args[:scalars] + tuple(
            pltpu.with_memory_space_constraint(x, pltpu.VMEM if i < resident else pltpu.HBM)
            for i, x in enumerate(args[scalars:])
        )
        specs = [pl.BlockSpec(memory_space=pltpu.SMEM)] * scalars
        specs += [pl.BlockSpec(memory_space=pltpu.VMEM)] * (len(args) - scalars)
        return pl.pallas_call(
            kernel,
            out_shape=[pltpu.HBM(o.shape, F32) if i in far else o for i, o in enumerate(outs)],
            in_specs=specs,
            out_specs=[pl.BlockSpec(memory_space=pltpu.VMEM)] * len(outs),
            scratch_shapes=list(scratch),
            compiler_params=pltpu.CompilerParams(vmem_limit_bytes=limit * 1024 * 1024),
            cost_estimate=CHEAP,
            name=name,
        )(*args)

    return run


def shards(
    vorticity, streamfunction, model_noise, offspring, footprint, observed, precision, block_rows
):
    groups, tiles = lax.axis_size("dom"), lax.axis_size("tile")
    members = offspring.shape[1]
    width = vorticity.shape[3]
    blocks = width // BW
    per = blocks // groups
    bands, observations, cells = footprint.shape[0], footprint.shape[2], footprint.shape[3]

    running = jnp.cumsum(offspring, axis=1)
    slots = jnp.arange(members, dtype=jnp.int32)
    parent = jnp.sum((running[:, None, :] <= slots[None, :, None]).astype(jnp.int32), axis=2)
    parent = jnp.minimum(parent, members - 1)
    edge = jnp.stack([lax.axis_index("tile"), jnp.int32(tiles)]).astype(jnp.int32)

    up = [(i, i + 1) for i in range(tiles - 1)]
    down = [(i + 1, i) for i in range(tiles - 1)]
    params = pltpu.CompilerParams(vmem_limit_bytes=VMEM_LIMIT)

    def pack(field, *noise):
        half = (MEM, LAYERS, SUB, width)
        return pl.pallas_call(
            functools.partial(pack_field, blocks=blocks, noisy=bool(noise)),
            grid=(2,),
            in_specs=[pl.BlockSpec(half, lambda i: (0, 0, i, 0))]
            + [pl.BlockSpec((1,) + half, lambda i: (0, 0, 0, i, 0))] * len(noise),
            out_specs=[
                pl.BlockSpec((SUB * FULL, BW), lambda i: (i, 0)),
                pl.BlockSpec((STEPS * FULL, BW), lambda i: (0, 0)),
                pl.BlockSpec((STEPS * FULL, BW), lambda i: (0, 0)),
            ],
            out_shape=[shape(ROWS * FULL, BW), shape(STEPS * FULL, BW), shape(STEPS * FULL, BW)],
            scratch_shapes=[pltpu.VMEM((SUB * FULL, BW), F32)],
            compiler_params=params,
            cost_estimate=CHEAP,
            name="pack_q" if noise else "pack_psi",
        )(field, *noise)

    p_main, p_up, p_down = pack(streamfunction)
    vorticity, p_up, p_down = lax.optimization_barrier((vorticity, p_up, p_down))
    p_below = lax.ppermute(p_up, "tile", up)
    p_above = lax.ppermute(p_down, "tile", down)
    q_main, q_up, q_down = pack(vorticity, model_noise)
    q_below = lax.ppermute(q_up, "tile", up)
    q_above = lax.ppermute(q_down, "tile", down)

    later_noise, p_below, p_above = lax.optimization_barrier((model_noise, p_below, p_above))
    noise = pl.pallas_call(
        functools.partial(pack_noise, groups=groups, per=per),
        grid=(1,),
        in_specs=[pl.BlockSpec((1, MEM, LAYERS, ROWS, width), lambda i: (1, 0, 0, 0, 0))],
        out_specs=pl.BlockSpec((groups, MEM, per * 4 + 1, SUB, BW), lambda i: (0, 0, 0, 0, 0)),
        out_shape=shape(groups, MEM, per * 4 + 1, SUB, BW),
        scratch_shapes=[pltpu.VMEM((ROWS * FULL, BW), F32)],
        compiler_params=params,
        cost_estimate=CHEAP,
        name="pack_noise",
    )(later_noise)
    noise, q_below, q_above = lax.optimization_barrier((noise, q_below, q_above))
    noise = lax.all_to_all(noise, "dom", split_axis=0, concat_axis=0, tiled=True)
    noise = noise.reshape(members, (per * 4 + 1) * SUB, BW)

    work = [
        pltpu.VMEM((DEEP * 4, PARTS * SUB, BW), F32),
        pltpu.VMEM((DEEP * 4, PARTS * SUB, BW), F32),
        pltpu.VMEM((8, PARTS * SUB, BW), F32),
        pltpu.VMEM((2 * ROWS * FULL, BW), F32),
    ]
    q_sent, p_sent = call(
        functools.partial(advance_members, groups=groups, per=per),
        [shape(groups, MEM, per * 4 + 1, SUB, BW)] * 2,
        work,
        scalars=1,
        resident=2,
        limit=32,
        far=(0, 1),
        name="advance_members",
    )(edge, q_main, p_main, q_below, p_below, q_above, p_above)
    beside = STEPS * 2 * HALF + 2 * members
    pieces = [shape(ROWS * 2 * HALF, BW), shape(8 * members, BW), shape(beside, BW), shape(beside, BW)]

    def spread(sent):
        owned = lax.all_to_all(sent, "dom", split_axis=0, concat_axis=0, tiled=True)
        return owned.reshape(members, (per * 4 + 1) * SUB, BW)

    def exchange(owned, noise=()):
        extra = [] if noise else [shape(per, ROWS * members, BW)]
        main, edges, to_up, to_down, *surface = call(
            functools.partial(resample, members=members, per=per, noisy=len(noise)),
            pieces + extra,
            [pltpu.VMEM((ROWS * FULL, BW), F32)],
            scalars=1,
            far=() if noise else (0, 1, 4),
            name="resample_q" if noise else "resample_psi",
        )(parent[0], owned, *noise)
        below = lax.ppermute(to_up, "tile", up)
        above = lax.ppermute(to_down, "tile", down)
        return main, edges, below, above, *surface

    p_sent, noise = lax.optimization_barrier((p_sent, noise))
    p_owned = spread(p_sent)
    q_sent, p_owned = lax.optimization_barrier((q_sent, p_owned))
    q_owned = spread(q_sent)
    p_main, p_edge, p_below, p_above, surface = exchange(p_owned)
    q_main, q_edge, q_below, q_above = exchange(q_owned, (noise,))

    stored = pltpu.with_memory_space_constraint(footprint, pltpu.HBM)

    def likelihood(cycle, surface, logs):
        small = pl.BlockSpec((1, per, observations), lambda a, c: (a, 0, 0))
        table = pl.BlockSpec((SUB, members), lambda a, c: (0, 0))
        return pl.pallas_call(
            functools.partial(score, members=members, cycle=cycle),
            grid=(bands, per),
            in_specs=[
                pl.BlockSpec(memory_space=pltpu.SMEM),
                pl.BlockSpec((per, ROWS * members, BW), lambda a, c: (0, 0, 0)),
                pl.BlockSpec((1, 1, observations, cells), lambda a, c: (a, c, 0, 0)),
                small,
                small,
                table,
            ],
            out_specs=table,
            out_shape=shape(SUB, members),
            scratch_shapes=[
                pltpu.VMEM((2 * members, cells), jnp.bfloat16),
                pltpu.VMEM((members, observations), F32),
            ],
            compiler_params=params,
            cost_estimate=CHEAP,
            name="score",
        )(block_rows, surface, stored, observed, precision, logs)

    logs = likelihood(0, surface, jnp.zeros((SUB, members), F32))
    p_main, logs = lax.optimization_barrier((p_main, logs))

    back, surface = call(
        functools.partial(advance_columns, members=members, per=per),
        [shape(members, per * 8, SUB, BW), shape(per, ROWS * members, BW)],
        work + [pltpu.VMEM((members // SUB * 2, BW, BW), F32)],
        scalars=2,
        limit=32,
        far=(0,),
        name="advance_columns",
    )(edge, parent[1], q_main, p_main, q_edge, p_edge, q_below, p_below, q_above, p_above)
    back = back.reshape(groups, MEM, per * 64, BW)
    mine = lax.all_to_all(back, "dom", split_axis=0, concat_axis=0, tiled=True)
    loglik = likelihood(1, surface, logs)

    q_out, psi_out = call(
        functools.partial(unpack_state, groups=groups, per=per),
        [shape(MEM, LAYERS, ROWS, width)] * 2,
        limit=12,
        name="unpack_state",
    )(mine)

    for axis, size in (("tile", tiles), ("dom", groups)):
        hop = 1
        while hop < size:
            def beside(step, value=loglik, axis=axis, size=size):
                return lax.ppermute(value, axis, [(i, i ^ step) for i in range(size)])

            if hop == 1 and (size.bit_length() - 1) % 2:
                loglik = loglik + beside(1)
                hop = 2
            else:
                loglik = (loglik + beside(hop)) + (beside(2 * hop) + beside(3 * hop))
                hop *= 4
    loglik = loglik[:CYCLES]
    total_obs = observed.size * groups * tiles
    mean_loglik = loglik / total_obs
    highest = jnp.max(loglik, axis=1, keepdims=True)
    scaled = jnp.exp(loglik - highest)
    weights = scaled / jnp.sum(scaled, axis=1, keepdims=True)
    return (q_out, psi_out, mean_loglik, weights)


def solution(mesh):
    return jax.shard_map(
        shards,
        mesh=mesh,
        in_specs=(
            P("dom", None, "tile", None),
            P("dom", None, "tile", None),
            P(None, "dom", None, "tile", None),
            P(),
            P("tile", "dom", None, None),
            P("tile", "dom", None),
            P("tile", "dom", None),
            P("tile", "dom"),
        ),
        out_specs=(P("dom", None, "tile", None), P("dom", None, "tile", None), P(), P()),
        check_vma=False,
    )
```
